128 devices in a mesh: slab: 16 (over x_lo, y, core), col: 8 (over z, x_hi).
Axes of the slice: x: 4 (x_hi: 2, x_lo: 2; x = x_hi * 2 + x_lo), y: 4, z: 4, core: 2. Of those that a mesh axis runs over, the one named last changes fastest.
Arguments:
- rest_points: float32 [3, 16, 16, 128], P(None, 'slab', 'col'), may hold values from 0 to 16, as said below
- tile_fill: int32 [16, 16], P('slab', 'col'), may hold values from 32 to 128, as said below
- displacement: float32 [3, 16, 16, 128], P(None, 'slab', 'col'), may hold values from -0.6 to 0.6
- velocity: float32 [3, 16, 16, 128], P(None, 'slab', 'col'), may hold values from -0.6 to 0.6
- back_extension: bfloat16 [2, 16, 16, 9, 128, 128], P(None, 'slab', 'col'), may hold values from -0.59765625 to 0.59765625
Outputs:
- displacement_out: float32 [3, 16, 16, 128], P(None, 'slab', 'col')
- velocity_out: float32 [3, 16, 16, 128], P(None, 'slab', 'col')
- back_extension_out: bfloat16 [2, 16, 16, 9, 128, 128], P(None, 'slab', 'col')
The draws below stay inside these ranges and needn't reach their ends.
Inputs may be any that keep to these rules, and one draw needn't show every extreme that they name: `tile_fill`: point slots of a tile are filled from the first one; at least a quarter of the 128 slots are live. `rest_points`: the points of tile (r, c) lie in its unit box: r plus [0, 1) along the first component, c plus [0, 1) along the second, [0, 1) along the third.
All inputs are finite; a program needn't handle non-finite values.
Results may differ from the reference program's by a relative error of at most 0.0051.
Values sent between devices are 32-bit elements; how exact they have to be, the bound alone decides.
No kernel may reach another device: no remote copies, remote signals or barrier semaphores. Data moves between devices by JAX's collectives and lax.ppermute only.
A program may use at most 128 MiB of HBM per device.

```python
import jax
import jax.numpy as jnp
from jax import lax

POINTS = 128
STEPS = 2
ROWS_ALL = 16
COLS_ALL = 16


def draw_rest_points(key, part):
    spread = jax.random.uniform(key, (3, ROWS_ALL, COLS_ALL, POINTS), jnp.float32)
    row_base = jnp.arange(ROWS_ALL, dtype=jnp.float32)[:, None, None]
    col_base = jnp.arange(COLS_ALL, dtype=jnp.float32)[None, :, None]
    return jnp.stack([row_base + spread[0], col_base + spread[1], spread[2]], 0)


def draw_tile_fill(key, part):
    counts = jax.random.randint(jax.random.fold_in(key, 7), (ROWS_ALL, COLS_ALL), POINTS // 4, POINTS + POINTS // 4 + 1)
    return jnp.minimum(counts, POINTS).astype(jnp.int32)


def levels(own_key, shape, split, smallest, high):
    def one(axis_at, blocks):
        steps = jax.random.uniform(jax.random.fold_in(jax.random.fold_in(own_key, 6), axis_at), (blocks,), jnp.float32, smallest / len(split), high / len(split))
        return jnp.repeat(jnp.exp(steps), shape[axis_at] // blocks).reshape((-1,) + (1,) * (len(shape) - axis_at - 1))

    loudness = one(*split[0])
    for cut in split[1:]:
        loudness = loudness * one(*cut)
    return loudness


def gaussian(rng, extent, width, bound, pieces=(), kind=jnp.bfloat16):
    gain = levels(rng, extent, pieces, -0.22, 0.18) if pieces else 1.0
    values = jax.random.normal(rng, extent, jnp.float32) * width * gain
    return jnp.minimum(jnp.maximum(values, -bound), bound).astype(kind)


def setup_inputs(seed: int = 0) -> dict:
    key_of = jax.random.split(jax.random.key(seed), 6)
    rest_points = draw_rest_points(jax.random.fold_in(key_of[5], 71), 0)
    tile_fill = draw_tile_fill(jax.random.fold_in(key_of[5], 71), 0)
    displacement = gaussian(key_of[2], (3, ROWS_ALL, COLS_ALL, POINTS), 0.1, 0.6, ((1, 16), (2, 8)), jnp.float32)
    velocity = gaussian(key_of[3], (3, ROWS_ALL, COLS_ALL, POINTS), 0.1, 0.6, ((1, 16), (2, 8)), jnp.float32)
    back_extension = gaussian(key_of[4], (2, ROWS_ALL, COLS_ALL, 9, POINTS, POINTS), 0.1, 0.59765625, ((1, 16), (2, 8)))
    return dict(rest_points=rest_points, tile_fill=tile_fill, displacement=displacement, velocity=velocity, back_extension=back_extension)


stencil_offsets = [(-1, -1), (-1, 0), (-1, 1), (0, -1), (0, 0), (0, 1), (1, -1), (1, 0), (1, 1)]

def pad_tiles(values, first):
    widths = [(0, 0)] * values.ndim
    widths[first] = (1, 1)
    widths[first + 1] = (1, 1)
    return jnp.pad(values, widths)

def pair_geometry(rest_halo, alive_halo, rows, cols, row_shift, col_shift):
    home_side = rest_halo[:, 1:1 + rows, 1:1 + cols, :, None]
    far_side = rest_halo[:, 1 + row_shift:1 + row_shift + rows, 1 + col_shift:1 + col_shift + cols, None, :]
    bond = far_side - home_side
    length = jnp.sqrt(lax.optimization_barrier(jnp.sum(bond * bond, axis=0)))
    closeness = jnp.maximum(1.0 - length, 0.0)
    weight = closeness * closeness * alive_halo[1:1 + rows, 1:1 + cols, :, None]
    weight = weight * alive_halo[1 + row_shift:1 + row_shift + rows, 1 + col_shift:1 + col_shift + cols, None, :]
    if row_shift == 0 and col_shift == 0:
        weight = weight * (1.0 - jnp.eye(weight.shape[-1], dtype=jnp.float32))
    return (length, weight)

def deformed(place_halo, length, rows, cols, row_shift, col_shift):
    home_side = place_halo[:, 1:1 + rows, 1:1 + cols, :, None]
    far_side = place_halo[:, 1 + row_shift:1 + row_shift + rows, 1 + col_shift:1 + col_shift + cols, None, :]
    separation = far_side - home_side
    squared = lax.optimization_barrier(jnp.sum(separation * separation, axis=0))
    stretch = jnp.sqrt(squared) - length
    bearing = separation * jax.lax.rsqrt(squared + 0.01)
    return (stretch, bearing)

def reference(rest_points, tile_fill, displacement, velocity, back_extension):
    rows, cols, points = (rest_points.shape[1], rest_points.shape[2], rest_points.shape[3])
    alive = (jnp.arange(points, dtype=jnp.int32)[None, None, :] < tile_fill[:, :, None]).astype(jnp.float32)
    rest_halo = pad_tiles(rest_points, 1)
    alive_halo = pad_tiles(alive, 0)
    geometry = [pair_geometry(rest_halo, alive_halo, rows, cols, rs, cs) for rs, cs in stencil_offsets]
    volume = jnp.zeros((rows, cols, points), jnp.float32)
    for length, weight in geometry:
        volume = volume + lax.optimization_barrier(jnp.sum(weight * length * length, axis=-1))
    volume = jnp.maximum(volume, 1.0)
    history = back_extension
    for step_index in range(STEPS):
        place_halo = rest_halo + pad_tiles(displacement, 1)
        shapes = [deformed(place_halo, geometry[index][0], rows, cols, rs, cs) for index, (rs, cs) in enumerate(stencil_offsets)]
        dilatation = jnp.zeros((rows, cols, points), jnp.float32)
        for index in range(9):
            length, weight = geometry[index]
            dilatation = dilatation + lax.optimization_barrier(jnp.sum(weight * length * shapes[index][0], axis=-1))
        dilatation = 3.0 * dilatation / volume
        forces, first_states, second_states = ([], [], [])
        for index in range(9):
            length, weight = geometry[index]
            deviator = shapes[index][0] - dilatation[..., None] * length / 3.0
            back_one = 0.6 * history[0, :, :, index].astype(jnp.float32) + 0.4 * deviator
            back_two = 0.95 * history[1, :, :, index].astype(jnp.float32) + 0.05 * deviator
            bond_force = 3.0 * dilatation[..., None] * weight * length / volume[..., None]
            bond_force = bond_force + 7.5 * weight / volume[..., None] * (0.4 * deviator + 0.35 * (deviator - back_one) + 0.25 * (deviator - back_two))
            forces.append(bond_force)
            first_states.append(back_one)
            second_states.append(back_two)
        history = jnp.stack([jnp.stack(first_states, 2), jnp.stack(second_states, 2)], 0).astype(jnp.bfloat16)
        force_halo = pad_tiles(jnp.stack(forces, 0), 1)
        total_force = jnp.zeros((3, rows, cols, points), jnp.float32)
        for index, (rs, cs) in enumerate(stencil_offsets):
            reverse = force_halo[8 - index, 1 + rs:1 + rs + rows, 1 + cs:1 + cs + cols]
            reverse = jnp.swapaxes(reverse, -1, -2)
            total_force = total_force + lax.optimization_barrier(jnp.sum((forces[index] + reverse)[None] * shapes[index][1], axis=-1))
        velocity = velocity + 0.2 * total_force
        displacement = displacement + 0.2 * velocity
    return (displacement, velocity, history)
```

```python
import functools

import jax
import jax.numpy as jnp
from jax import lax
from jax.experimental import pallas as pl
from jax.experimental.pallas import tpu as pltpu
from jax.sharding import PartitionSpec as P

OFFSETS = [(-1, -1), (-1, 0), (-1, 1), (0, -1), (0, 0), (0, 1), (1, -1), (1, 0), (1, 1)]
LANES = 128
CHUNK = 16
DEAD = -1e9


def root(squared):
    return squared * lax.rsqrt(jnp.maximum(squared, 1e-36))


def step_kernel(first, *refs):
    if first:
        halo, old, push, new, rows, cols, geo, coef, row_sum, col_sum = refs
    else:
        halo, pull, old, push, new, own, rows, cols, geo, coef, row_sum, col_sum = refs
    for r in range(3):
        for c in range(4):
            rest, disp = halo[r, c, 0:3], halo[r, c, 3:6]
            alive = halo[r, c, 9:10]
            if not first:
                speed = halo[r, c, 6:9] + 0.2 * (pull[r, 4 * c : 4 * c + 3] * alive)
                disp = disp + 0.2 * speed
                if r == 1 and c in (1, 2):
                    own[c - 1, 0:3] = disp
                    own[c - 1, 3:6] = speed
            t = r * 4 + c
            rows[t, 0:3] = rest
            rows[t, 3:6] = rest + disp
            rows[t, 6:7] = jnp.where(alive > 0.5, 1.0, DEAD)
            rows[t, 7:8] = alive
    for h in range(2):
        cols[h] = jnp.transpose(rows[5 + h])
    col_sum[...] = jnp.zeros_like(col_sum)

    for h in range(2):

        def measure(i, carry, h=h):
            at = pl.ds(pl.multiple_of(i * CHUNK, CHUNK), CHUNK)
            home = [jnp.broadcast_to(cols[h, at, j : j + 1], (CHUNK, LANES)) for j in range(6)]
            here = cols[h, at, 7:8]
            volume = jnp.zeros((CHUNK, LANES), jnp.float32)
            swell = jnp.zeros((CHUNK, LANES), jnp.float32)
            for k, (dr, dc) in enumerate(OFFSETS):
                t = (1 + dr) * 4 + 1 + h + dc
                bond = [rows[t, j : j + 1] - home[j] for j in range(3)]
                length = root(bond[0] * bond[0] + bond[1] * bond[1] + bond[2] * bond[2])
                close = jnp.maximum(rows[t, 6:7] - length, 0.0)
                weight = close * close
                gap = [rows[t, 3 + j : 4 + j] - home[3 + j] for j in range(3)]
                squared = gap[0] * gap[0] + gap[1] * gap[1] + gap[2] * gap[2]
                stretch = root(squared) - length
                lever = weight * length
                volume = volume + lever * length
                swell = swell + lever * stretch
                geo[0, h * 9 + k, at] = length
                geo[1, h * 9 + k, at] = weight
                geo[2, h * 9 + k, at] = stretch
                geo[3, h * 9 + k, at] = lax.rsqrt(squared + 0.01)
            mass = jnp.maximum(here * jnp.sum(volume, axis=1, keepdims=True), 1.0)
            dilatation = 3.0 * (here * jnp.sum(swell, axis=1, keepdims=True)) / mass
            share = here / mass
            coef[3 * h, at] = jnp.broadcast_to(dilatation / 3.0, (CHUNK, LANES))
            coef[3 * h + 1, at] = jnp.broadcast_to(3.0 * dilatation * share, (CHUNK, LANES))
            coef[3 * h + 2, at] = jnp.broadcast_to(7.5 * share, (CHUNK, LANES))
            return carry

        lax.fori_loop(0, LANES // CHUNK, measure, 0)

    for h in range(2):

        def push_pull(i, carry, h=h):
            at = pl.ds(pl.multiple_of(i * CHUNK, CHUNK), CHUNK)
            home = [jnp.broadcast_to(cols[h, at, j : j + 1], (CHUNK, LANES)) for j in range(3, 6)]
            third, bulk, shear = coef[3 * h, at], coef[3 * h + 1, at], coef[3 * h + 2, at]
            total = [jnp.zeros((CHUNK, LANES), jnp.float32) for _ in range(3)]
            for k, (dr, dc) in enumerate(OFFSETS):
                t = (1 + dr) * 4 + 1 + h + dc
                length = geo[0, h * 9 + k, at]
                deviator = geo[2, h * 9 + k, at] - third * length
                one = old[0, 0, h, k, at].astype(jnp.float32)
                two = old[1, 0, h, k, at].astype(jnp.float32)
                new[0, 0, h, k, at] = (0.6 * one + 0.4 * deviator).astype(jnp.bfloat16)
                new[1, 0, h, k, at] = (0.95 * two + 0.05 * deviator).astype(jnp.bfloat16)
                mixed = 0.8475 * deviator - 0.21 * one - 0.2375 * two
                force = geo[1, h * 9 + k, at] * (length * bulk + shear * mixed)
                force = force * geo[3, h * 9 + k, at]
                for j in range(3):
                    part = force * (rows[t, 3 + j : 4 + j] - home[j])
                    total[j] = total[j] + part
                    col_sum[3 * t + j] += part[0:8] + part[8:16]
            for j in range(3):
                row_sum[3 * h + j, at] = total[j]
            return carry

        lax.fori_loop(0, LANES // CHUNK, push_pull, 0)

    ones = jnp.ones((8, LANES), jnp.float32)
    for r in range(3):
        for c in range(4):
            t = r * 4 + c
            for j in range(3):
                value = -jnp.sum(col_sum[3 * t + j], axis=0, keepdims=True)
                if r == 1 and c in (1, 2):
                    sums = lax.dot_general(
                        ones,
                        row_sum[3 * (c - 1) + j],
                        (((1,), (1,)), ((), ())),
                        precision=lax.Precision.HIGHEST,
                        preferred_element_type=jnp.float32,
                    )
                    value = value + sums[0:1]
                push[r, 4 * c + j : 4 * c + j + 1] = value
            push[r, 4 * c + 3 : 4 * c + 4] = jnp.zeros((1, LANES), jnp.float32)


def run_step(first, operands, history):
    f32 = jnp.float32
    outs = [jax.ShapeDtypeStruct((3, 16, LANES), f32), jax.ShapeDtypeStruct(history.shape, history.dtype)]
    if not first:
        outs.append(jax.ShapeDtypeStruct((2, 6, LANES), f32))
    vmem = pl.BlockSpec(memory_space=pltpu.VMEM)
    return pl.pallas_call(
        functools.partial(step_kernel, first),
        out_shape=outs,
        in_specs=[vmem] * (len(operands) + 1),
        out_specs=[vmem] * len(outs),
        scratch_shapes=[
            pltpu.VMEM((12, 8, LANES), f32),
            pltpu.VMEM((2, LANES, 8), f32),
            pltpu.VMEM((4, 18, LANES, LANES), f32),
            pltpu.VMEM((6, LANES, LANES), f32),
            pltpu.VMEM((6, LANES, LANES), f32),
            pltpu.VMEM((36, 8, LANES), f32),
        ],
        compiler_params=pltpu.CompilerParams(vmem_limit_bytes=24 * 1024 * 1024),
        name="step_one" if first else "step_two",
    )(*operands, history)


def swap_pairs(size, parity):
    pairs = []
    for i in range(size):
        pairs.append((i, (i + 1) % size if i % 2 == parity else (i - 1) % size))
    return pairs


def per_device(slabs, columns, rest_points, tile_fill, displacement, velocity, back_extension):
    s, c = lax.axis_index("slab"), lax.axis_index("col")
    s_odd, c_odd = s % 2 == 1, c % 2 == 1
    slab_near, slab_far = swap_pairs(slabs, 0), swap_pairs(slabs, 1)
    col_near, col_far = swap_pairs(columns, 0), swap_pairs(columns, 1)

    alive = (jnp.arange(LANES, dtype=jnp.int32)[None, None, :] < tile_fill[0][:, None, None]).astype(jnp.float32)
    own = jnp.concatenate(
        [jnp.swapaxes(a[:, 0], 0, 1) for a in (rest_points, displacement, velocity)]
        + [alive, jnp.zeros((2, 6, LANES), jnp.float32)],
        axis=1,
    )
    near = lax.ppermute(own, "slab", slab_near)
    far = lax.ppermute(own, "slab", slab_far)
    before = jnp.where(s > 0, jnp.where(s_odd, near, far), 0.0)
    after = jnp.where(s < slabs - 1, jnp.where(s_odd, far, near), 0.0)
    tiles = jnp.stack([before, own, after])
    near = lax.ppermute(jnp.where(c_odd, tiles[:, 0], tiles[:, 1]), "col", col_near)
    far = lax.ppermute(jnp.where(c_odd, tiles[:, 1], tiles[:, 0]), "col", col_far)
    left = jnp.where(c > 0, jnp.where(c_odd, near, far), 0.0)
    right = jnp.where(c < columns - 1, jnp.where(c_odd, far, near), 0.0)
    halo = jnp.stack([left, tiles[:, 0], tiles[:, 1], right], 1)

    def across(sums):
        half_l, half_r = sums[..., :8, :], sums[..., 8:, :]
        near = lax.ppermute(jnp.where(c_odd, half_l, half_r), "col", col_near)
        far = lax.ppermute(jnp.where(c_odd, half_r, half_l), "col", col_far)
        half_l = half_l + jnp.where(c_odd, near, far)
        half_r = half_r + jnp.where(c_odd, far, near)
        return jnp.concatenate([half_l, half_r], axis=-2)

    push, history = run_step(True, (halo,), back_extension)
    got = lax.ppermute(jnp.where(s_odd, push[0], push[2]), "slab", slab_near)
    two = jnp.where(s_odd, jnp.stack([push[1] + got, push[2]]), jnp.stack([push[0], push[1] + got]))
    two = two + lax.ppermute(two, "slab", slab_far)
    got = lax.ppermute(jnp.where(s_odd, two[0], two[1]), "slab", slab_near)
    three = jnp.where(s_odd, jnp.stack([got, two[0], two[1]]), jnp.stack([two[0], two[1], got]))
    pull = across(three)

    push, history, state = run_step(False, (halo, pull), history)
    near = lax.ppermute(jnp.where(s_odd, push[0], push[2]), "slab", slab_near)
    far = lax.ppermute(jnp.where(s_odd, push[2], push[0]), "slab", slab_far)
    total = across(push[1] + near + far)
    total = jnp.stack([total[4:7], total[8:11]], axis=1)
    state = jnp.swapaxes(state, 0, 1)
    velocity = state[3:6] + 0.2 * total
    displacement = state[0:3] + 0.2 * velocity
    return (displacement[:, None], velocity[:, None], history)


def solution(mesh):
    in_specs = (
        P(None, "slab", "col", None),
        P("slab", "col"),
        P(None, "slab", "col", None),
        P(None, "slab", "col", None),
        P(None, "slab", "col", None, None, None),
    )
    out_specs = (
        P(None, "slab", "col", None),
        P(None, "slab", "col", None),
        P(None, "slab", "col", None, None, None),
    )
    return jax.shard_map(
        functools.partial(per_device, mesh.shape["slab"], mesh.shape["col"]),
        mesh=mesh,
        in_specs=in_specs,
        out_specs=out_specs,
        check_vma=False,
    )
```

```python
import functools

import jax
import jax.numpy as jnp
from jax import lax
from jax.experimental import pallas as pl
from jax.experimental.pallas import tpu as pltpu
from jax.sharding import PartitionSpec as P

OFFSETS = [(-1, -1), (-1, 0), (-1, 1), (0, -1), (0, 0), (0, 1), (1, -1), (1, 0), (1, 1)]
N = 128
CHUNK = 16
F32 = jnp.float32
VMEM = pl.BlockSpec(memory_space=pltpu.VMEM)
PAIRS = [(h, k) for h in range(2) for k in range(9)]
INNER = [(h, k) for h, k in PAIRS if 0 <= h + OFFSETS[k][1] <= 1]
OUTER = [(h, k) for h, k in PAIRS if not 0 <= h + OFFSETS[k][1] <= 1]


def root(squared):
    return squared * lax.rsqrt(jnp.maximum(squared, 1e-36))


def block(*shape):
    return jax.ShapeDtypeStruct(shape, F32)


def call(body, name, outs, operands, scratch=(), specs=None, work=0, limit=24):
    cost = pl.CostEstimate(flops=work, bytes_accessed=1 << 16, transcendentals=0) if work else None
    return pl.pallas_call(
        body,
        out_shape=outs,
        in_specs=specs or [VMEM] * len(operands),
        out_specs=[VMEM] * len(outs),
        scratch_shapes=list(scratch),
        compiler_params=pltpu.CompilerParams(vmem_limit_bytes=limit and limit * 1024 * 1024),
        cost_estimate=cost,
        name=name,
    )(*operands)


def each_chunk(body, unroll=1):
    def step(i, carry):
        body(pl.ds(pl.multiple_of(i * CHUNK, CHUNK), CHUNK))
        return carry

    lax.fori_loop(0, N // CHUNK, step, 0, unroll=unroll)


def across(ref, at, j):
    return jnp.broadcast_to(ref[at, j : j + 1], (CHUNK, N))


def pack_body(fill_far, rest_far, displacement_far, velocity_far, own, state, fill, rest, displacement, velocity, sems):
    pairs = ((fill_far, fill), (rest_far, rest), (displacement_far, displacement), (velocity_far, velocity))
    copies = [pltpu.make_async_copy(a, b, sems.at[i]) for i, (a, b) in enumerate(pairs)]
    for copy in copies:
        copy.start()
    for copy in copies:
        copy.wait()
    lane = lax.broadcasted_iota(jnp.int32, (1, N), 1)
    for t in range(2):
        for j in range(3):
            spot, shift = rest[j, 0, t : t + 1], displacement[j, 0, t : t + 1]
            speed = velocity[j, 0, t : t + 1]
            own[t, j : j + 1] = spot
            own[t, 3 + j : 4 + j] = spot + shift
            state[t, j : j + 1] = shift + 0.2 * speed
            state[t, 3 + j : 4 + j] = speed
        own[t, 6:7] = jnp.where(lane < fill[0, t], 1.0, 0.0)
        own[t, 7:8] = jnp.ones((1, N), F32)
        state[t, 6:8] = jnp.zeros((2, N), F32)


def recall_body(far, held, mixed, sems):
    copies = {}
    for h in range(2):
        for j in range(2):
            copies[j, h] = pltpu.make_async_copy(far.at[j, 0, h], held.at[j, 0, h], sems.at[j, h])
            copies[j, h].start()
    for h in range(2):
        copies[0, h].wait()
        copies[1, h].wait()

        def body(at, h=h):
            for k in range(9):
                one, two = held[0, 0, h, k, at].astype(F32), held[1, 0, h, k, at].astype(F32)
                mixed[9 * h + k, at] = 0.21 * one + 0.2375 * two

        each_chunk(body)


def measure(at, blocks, target, home, mixed, volume, swell, length_, lever_, weight_, pull_, rest_, stretch_):
    for n, (h, k) in enumerate(blocks):
        t = target(h, k)
        bond = [t[j : j + 1] - home[h][j] for j in range(3)]
        length = root(bond[0] * bond[0] + bond[1] * bond[1] + bond[2] * bond[2])
        close = jnp.maximum(t[6:7] - length, 0.0)
        weight = close * close
        gap = [t[3 + j : 4 + j] - home[h][3 + j] for j in range(3)]
        squared = gap[0] * gap[0] + gap[1] * gap[1] + gap[2] * gap[2]
        stretch = root(squared) - length
        lever = weight * length
        volume[h] = volume[h] + lever * length
        swell[h] = swell[h] + lever * stretch
        length_[n, at] = length
        lever_[n, at] = lever
        weight_[n, at] = weight
        pull_[n, at] = weight * lax.rsqrt(squared + 0.01)
        rest_[n, at] = 0.8475 * stretch - mixed[9 * h + k, at]
        stretch_[n, at] = stretch


def inner_body(tiles, mixed, cols, volume_, swell_, *geo):
    for h in range(2):
        cols[h] = jnp.transpose(tiles[1, h])

    def target(h, k):
        return tiles.at[1 + OFFSETS[k][0], h + OFFSETS[k][1]]

    def body(at):
        home = [[across(cols.at[h], at, j) for j in range(6)] for h in range(2)]
        volume = [jnp.zeros((CHUNK, N), F32)] * 2
        swell = [jnp.zeros((CHUNK, N), F32)] * 2
        measure(at, INNER, target, home, mixed, volume, swell, *geo)
        for h in range(2):
            volume_[h, at] = volume[h]
            swell_[h, at] = swell[h]

    each_chunk(body)


def side(left, right, r, h):
    return right.at[r] if h else left.at[r]


def force_sums(pulls, gaps, push, row_sum, col_sum, base):
    lane = lax.broadcasted_iota(jnp.int32, (N, N), 1)
    table = jnp.zeros((N, N), F32)
    for q in range(6):
        table = jnp.where(lane == q, jnp.sum(row_sum[q], axis=1, keepdims=True), table)
    table = jnp.transpose(table)
    for r in range(3):
        for c in range(4):
            for j in range(3):
                value = -jnp.sum(col_sum[12 * r + 3 * c + j], axis=0, keepdims=True)
                if r == 1 and c in (1, 2):
                    q = 3 * (c - 1) + j
                    value = value + table[q : q + 1]
                if base is not None:
                    value = 0.04 * value
                    if r == 1 and c in (1, 2):
                        value = value + base[c - 1, j : j + 1]
                push[r, 4 * c + j : 4 * c + j + 1] = value
            push[r, 4 * c + 3 : 4 * c + 4] = jnp.zeros((1, N), F32)


def add_force(at, h, k, force, gap, total, col_sum):
    t = (1 + OFFSETS[k][0]) * 4 + 1 + h + OFFSETS[k][1]
    for j in range(3):
        part = force * gap[j]
        total[h][j] = total[h][j] + part
        col_sum[3 * t + j] += part[0:8] + part[8:16]


def first_body(tiles, left, right, mixed, state, cols, volume_, swell_, *refs):
    inner, (push, third_, shear_), refs = refs[:6], refs[6:9], refs[9:]
    outer, (vol, swl, bulk, row_sum, col_sum) = refs[:6], refs[6:]

    def measure_outer(at):
        home = [[across(cols.at[h], at, j) for j in range(6)] for h in range(2)]
        volume = [volume_[h, at] for h in range(2)]
        swell = [swell_[h, at] for h in range(2)]
        measure(
            at, OUTER, lambda h, k: side(left, right, 1 + OFFSETS[k][0], h), home, mixed, volume, swell, *outer
        )
        for h in range(2):
            vol[h, at] = volume[h]
            swl[h, at] = swell[h]

    each_chunk(measure_outer)
    for h in range(2):
        here = cols[h, :, 6:7]
        mass = jnp.maximum(here * jnp.sum(vol[h], axis=1, keepdims=True), 1.0)
        dilatation = 3.0 * (here * jnp.sum(swl[h], axis=1, keepdims=True)) / mass
        shear = 7.5 * here / mass
        third_[h] = jnp.broadcast_to(dilatation / 3.0, (N, N))
        shear_[h] = jnp.broadcast_to(shear, (N, N))
        bulk[h] = jnp.broadcast_to(0.1175 * dilatation * shear, (N, N))
    col_sum[...] = jnp.zeros_like(col_sum)

    def forces(at):
        total = [[jnp.zeros((CHUNK, N), F32)] * 3 for _ in range(2)]
        for h in range(2):
            home = [across(cols.at[h], at, 3 + j) for j in range(3)]
            flat, tall = shear_[h, at], bulk[h, at]
            for k, (dr, dc) in enumerate(OFFSETS):
                if (h, k) in INNER:
                    geo, n, t = inner, INNER.index((h, k)), tiles.at[1 + dr, h + dc]
                else:
                    geo, n, t = outer, OUTER.index((h, k)), side(left, right, 1 + dr, h)
                force = geo[3][n, at] * (geo[0][n, at] * tall + geo[4][n, at] * flat)
                gap = [t[3 + j : 4 + j] - home[j] for j in range(3)]
                add_force(at, h, k, force, gap, total, col_sum)
            for j in range(3):
                row_sum[3 * h + j, at] = total[h][j]

    each_chunk(forces)
    force_sums(None, None, push, row_sum, col_sum, state)


def relax_body(held, third, shear, len_i, len_o, wgt_i, wgt_o, str_i, str_o, new, mixed, firm):
    def body(at):
        for h in range(2):
            lean, flat = third[h, at], shear[h, at]
            for k in range(9):
                if (h, k) in INNER:
                    n, length, weight, stretch = INNER.index((h, k)), len_i, wgt_i, str_i
                else:
                    n, length, weight, stretch = OUTER.index((h, k)), len_o, wgt_o, str_o
                deviator = stretch[n, at] - lean * length[n, at]
                one = (0.6 * held[0, 0, h, k, at].astype(F32) + 0.4 * deviator).astype(jnp.bfloat16)
                two = (0.95 * held[1, 0, h, k, at].astype(F32) + 0.05 * deviator).astype(jnp.bfloat16)
                new[0, 0, h, k, at] = one
                new[1, 0, h, k, at] = two
                mixed[9 * h + k, at] = 0.21 * one.astype(F32) + 0.2375 * two.astype(F32)
                firm[9 * h + k, at] = weight[n, at] * flat

    each_chunk(body)


def second_body(tiles, left, right, pull, state, shear_, mixed, firm, len_i, len_o, lev_i, lev_o, *refs):
    push, third_, stretch_, own, rows, cols, swl, bulk, kernel_, rest_, row_sum, col_sum = refs
    for r in range(3):
        for c in range(4):
            t = tiles.at[r, c - 1] if c in (1, 2) else (right if c else left).at[r]
            shift = pull[r, 4 * c : 4 * c + 3] * t[7:8]
            rows[4 * r + c, 0:3] = t[0:3] + shift
            rows[4 * r + c, 3:8] = jnp.zeros((5, N), F32)
            if r == 1 and c in (1, 2):
                own[c - 1, 0:3] = shift
                own[c - 1, 3:6] = state[c - 1, 3:6] + 5.0 * (shift - state[c - 1, 0:3])
                own[c - 1, 6:8] = jnp.zeros((2, N), F32)
    for h in range(2):
        cols[h] = jnp.transpose(rows[5 + h])

    def lengths(h, k):
        if (h, k) in INNER:
            return INNER.index((h, k)), len_i, lev_i
        return OUTER.index((h, k)), len_o, lev_o

    def stretches(at):
        for h in range(2):
            home = [across(cols.at[h], at, j) for j in range(3)]
            swell = jnp.zeros((CHUNK, N), F32)
            for k, (dr, dc) in enumerate(OFFSETS):
                n, length, lever = lengths(h, k)
                t, m = (1 + dr) * 4 + 1 + h + dc, 9 * h + k
                gap = [rows[t, j : j + 1] - home[j] for j in range(3)]
                squared = gap[0] * gap[0] + gap[1] * gap[1] + gap[2] * gap[2]
                stretch = root(squared) - length[n, at]
                swell = swell + lever[n, at] * stretch
                stretch_[m, at] = stretch
                kernel_[m, at] = firm[m, at] * lax.rsqrt(squared + 0.01)
                rest_[m, at] = 0.8475 * stretch - mixed[m, at]
            swl[h, at] = swell

    each_chunk(stretches)
    for h in range(2):
        dilatation = 0.4 * shear_[h] * jnp.sum(swl[h], axis=1, keepdims=True)
        third_[h] = dilatation / 3.0
        bulk[h] = 0.1175 * dilatation
    col_sum[...] = jnp.zeros_like(col_sum)

    def forces(at):
        total = [[jnp.zeros((CHUNK, N), F32)] * 3 for _ in range(2)]
        for h in range(2):
            home = [across(cols.at[h], at, j) for j in range(3)]
            tall = bulk[h, at]
            for k, (dr, dc) in enumerate(OFFSETS):
                n, length, _ = lengths(h, k)
                t, m = (1 + dr) * 4 + 1 + h + dc, 9 * h + k
                force = kernel_[m, at] * (length[n, at] * tall + rest_[m, at])
                gap = [rows[t, j : j + 1] - home[j] for j in range(3)]
                add_force(at, h, k, force, gap, total, col_sum)
            for j in range(3):
                row_sum[3 * h + j, at] = total[h][j]

    each_chunk(forces)
    force_sums(None, None, push, row_sum, col_sum, None)


def settle_body(held, third, len_i, len_o, stretch, new):
    def body(at):
        for h in range(2):
            lean = third[h, at]
            for k in range(9):
                length = len_i[INNER.index((h, k)), at] if (h, k) in INNER else len_o[OUTER.index((h, k)), at]
                deviator = stretch[9 * h + k, at] - lean * length
                one, two = held[0, 0, h, k, at].astype(F32), held[1, 0, h, k, at].astype(F32)
                new[0, 0, h, k, at] = (0.6 * one + 0.4 * deviator).astype(jnp.bfloat16)
                new[1, 0, h, k, at] = (0.95 * two + 0.05 * deviator).astype(jnp.bfloat16)

    each_chunk(body)


def finish_body(total, own, displacement, velocity):
    for t in range(2):
        for j in range(3):
            q = 4 * (t + 1) + j
            speed = own[t, 3 + j : 4 + j] + 0.2 * total[q : q + 1]
            velocity[j, 0, t : t + 1] = speed
            displacement[j, 0, t : t + 1] = own[t, j : j + 1] + 0.2 * speed


def swap_pairs(size, parity):
    return [(i, (i + 1) % size if i % 2 == parity else (i - 1) % size) for i in range(size)]


def inner_swaps(slabs, columns):
    pairs = []
    for s in range(slabs):
        for c in range(columns):
            if c in (0, columns - 1):
                pairs.append((s * columns + c, (s ^ 1) * columns + c))
            else:
                pairs.append((s * columns + c, s * columns + (c + 1 if c % 2 else c - 1)))
    return pairs


def per_device(slabs, columns, rest_points, tile_fill, displacement, velocity, back_extension):
    s, c = lax.axis_index("slab"), lax.axis_index("col")
    s_odd, c_odd = s % 2 == 1, c % 2 == 1
    slab_near, slab_far = swap_pairs(slabs, 0), swap_pairs(slabs, 1)
    col_near, col_far = swap_pairs(columns, 0), inner_swaps(slabs, columns)

    def over_slab(to_near, to_far):
        return lax.ppermute(to_near, "slab", slab_near), lax.ppermute(to_far, "slab", slab_far)

    def over_col(to_left, to_right):
        near = lax.ppermute(jnp.where(c_odd, to_left, to_right), "col", col_near)
        far = lax.ppermute(jnp.where(c_odd, to_right, to_left), ("slab", "col"), col_far)
        from_left = jnp.where(c > 0, jnp.where(c_odd, near, far), 0.0)
        from_right = jnp.where(c < columns - 1, jnp.where(c_odd, far, near), 0.0)
        return from_left, from_right

    history = jax.ShapeDtypeStruct(back_extension.shape, back_extension.dtype)
    hbm = pl.BlockSpec(memory_space=pl.ANY)
    own, state = call(
        pack_body,
        "pack",
        [block(2, 8, N), block(2, 8, N)],
        (tile_fill, rest_points, displacement, velocity),
        scratch=[pltpu.SMEM(tile_fill.shape, jnp.int32)]
        + [pltpu.VMEM(rest_points.shape, F32)] * 3
        + [pltpu.SemaphoreType.DMA((4,))],
        specs=[hbm] * 4,
        limit=None,
    )
    near, far = over_slab(own, own)
    held, mixed = call(
        recall_body,
        "recall",
        [history, block(18, N, N)],
        (back_extension,),
        scratch=[pltpu.SemaphoreType.DMA((2, 2))],
        specs=[hbm],
        work=2_000_000,
    )
    near, far, held, mixed = lax.optimization_barrier((near, far, held, mixed))
    before = jnp.where(s > 0, jnp.where(s_odd, near, far), 0.0)
    after = jnp.where(s < slabs - 1, jnp.where(s_odd, far, near), 0.0)
    tiles = jnp.stack([before, own, after])
    left, right = over_col(tiles[:, 0], tiles[:, 1])
    cols, volume, swell, *inner = call(
        inner_body,
        "inner",
        [block(2, N, 8)] + [block(2, N, N)] * 2 + [block(12, N, N)] * 6,
        (tiles, mixed),
        work=6_000_000,
    )
    sums = [pltpu.VMEM((6, N, N), F32), pltpu.VMEM((36, 8, N), F32)]
    push, third, shear, *outer = call(
        first_body,
        "first",
        [block(3, 16, N), block(2, N, N), block(2, N, N)] + [block(6, N, N)] * 6,
        (tiles, left, right, mixed, state, cols, volume, swell, *inner),
        scratch=[pltpu.VMEM((2, N, N), F32)] * 3 + sums,
        work=8_000_000,
    )
    got = lax.ppermute(jnp.where(s_odd, push[0], push[2]), "slab", slab_near)
    two = jnp.where(s_odd, jnp.stack([push[1] + got, push[2]]), jnp.stack([push[0], push[1] + got]))
    back = lax.ppermute(two, "slab", slab_far)
    held, mixed, firm = call(
        relax_body,
        "relax",
        [history, block(18, N, N), block(18, N, N)],
        (held, third, shear, inner[0], outer[0], inner[2], outer[2], inner[5], outer[5]),
        work=4_000_000,
    )
    back, held, mixed, firm = lax.optimization_barrier((back, held, mixed, firm))
    two = two + back
    got = lax.ppermute(jnp.where(s_odd, two[0], two[1]), "slab", slab_near)
    three = jnp.where(s_odd, jnp.stack([got, two[0], two[1]]), jnp.stack([two[0], two[1], got]))
    lo, hi = three[:, :8], three[:, 8:]
    left_sum, right_sum = over_col(lo, hi)
    pull = jnp.concatenate([lo + left_sum, hi + right_sum], axis=1)

    push, third, stretch, own = call(
        second_body,
        "second",
        [block(3, 16, N), block(2, N, N), block(18, N, N), block(2, 8, N)],
        (tiles, left, right, pull, state, shear, mixed, firm, inner[0], outer[0], inner[1], outer[1]),
        scratch=[pltpu.VMEM((12, 8, N), F32), pltpu.VMEM((2, N, 8), F32)]
        + [pltpu.VMEM((2, N, N), F32)] * 2
        + [pltpu.VMEM((18, N, N), F32)] * 2
        + sums,
        work=8_000_000,
    )
    (held,) = call(settle_body, "settle", [history], (held, third, inner[0], outer[0], stretch), work=3_000_000)
    near, far = over_slab(jnp.where(s_odd, push[0], push[2]), jnp.where(s_odd, push[2], push[0]))
    total = push[1] + near + far
    lo, hi = total[:8], total[8:]
    left_sum, right_sum = over_col(lo, hi)
    total = jnp.concatenate([lo + left_sum, hi + right_sum], axis=0)
    shape = block(*rest_points.shape)
    displacement, velocity = call(finish_body, "finish", [shape, shape], (total, own))
    return (displacement, velocity, held)


def solution(mesh):
    in_specs = (
        P(None, "slab", "col", None),
        P("slab", "col"),
        P(None, "slab", "col", None),
        P(None, "slab", "col", None),
        P(None, "slab", "col", None, None, None),
    )
    out_specs = (
        P(None, "slab", "col", None),
        P(None, "slab", "col", None),
        P(None, "slab", "col", None, None, None),
    )
    return jax.shard_map(
        functools.partial(per_device, mesh.shape["slab"], mesh.shape["col"]),
        mesh=mesh,
        in_specs=in_specs,
        out_specs=out_specs,
        check_vma=False,
    )
```

```python
import functools

import jax
import jax.numpy as jnp
from jax import lax
from jax.experimental import pallas as pl
from jax.experimental.pallas import tpu as pltpu
from jax.sharding import PartitionSpec as P


N = 128
CHUNK = 16
F32 = jnp.float32
VMEM = pl.BlockSpec(memory_space=pltpu.VMEM)
BLOCKS = [(i, h, e) for i in range(3) for h in range(2) for e in range(3)]
INNER = [b for b in BLOCKS if 1 <= b[1] + b[2] <= 2]
OUTER = [b for b in BLOCKS if not 1 <= b[1] + b[2] <= 2]


def root(squared):
    return squared * lax.rsqrt(jnp.maximum(squared, 1e-36))


def block(*shape):
    return jax.ShapeDtypeStruct(shape, F32)


def call(body, outs, operands, scratch=(), specs=None, work=0, limit=24):
    cost = pl.CostEstimate(flops=work, bytes_accessed=1 << 16, transcendentals=0) if work else None
    return pl.pallas_call(
        body,
        out_shape=outs,
        in_specs=specs or [VMEM] * len(operands),
        out_specs=[VMEM] * len(outs),
        scratch_shapes=list(scratch),
        compiler_params=pltpu.CompilerParams(vmem_limit_bytes=limit and limit * 1024 * 1024),
        cost_estimate=cost,
    )(*operands)


def each_chunk(body):
    def step(i, carry):
        body(pl.ds(pl.multiple_of(i * CHUNK, CHUNK), CHUNK))
        return carry

    lax.fori_loop(0, N // CHUNK, step, 0)


def first_offset(i):
    odd = lax.axis_index("slab") % 2
    return (6 * (1 - odd), 3, 6 * odd)[i]


def spread(homes, h, tile, count):
    columns = jnp.transpose(tile)
    for j in range(count):
        homes[h, j] = jnp.broadcast_to(columns[:, j : j + 1], (N, N))


def either(inner, outer, i, h, e):
    if (i, h, e) in INNER:
        return inner, INNER.index((i, h, e))
    return outer, OUTER.index((i, h, e))


def tile_of(tiles, left, right, i, h, e):
    c = h + e
    return tiles.at[i, c - 1] if c in (1, 2) else (right if c else left).at[i]


def pack_body(fill_far, rest_far, displacement_far, velocity_far, own, state, fill, rest, displacement, velocity, sems):
    pairs = ((fill_far, fill), (rest_far, rest), (displacement_far, displacement), (velocity_far, velocity))
    copies = [pltpu.make_async_copy(a, b, sems.at[i]) for i, (a, b) in enumerate(pairs)]
    for copy in copies:
        copy.start()
    for copy in copies:
        copy.wait()
    lane = lax.broadcasted_iota(jnp.int32, (1, N), 1)
    state[...] = jnp.zeros_like(state)
    for t in range(2):
        for j in range(3):
            spot, shift = rest[j, 0, t : t + 1], displacement[j, 0, t : t + 1]
            speed = velocity[j, 0, t : t + 1]
            own[t, j : j + 1] = spot
            own[t, 3 + j : 4 + j] = spot + shift
            state[0, 4 * t + 4 + j : 4 * t + 5 + j] = shift + 0.2 * speed
            state[1, 4 * t + 4 + j : 4 * t + 5 + j] = speed
        own[t, 6:7] = jnp.where(lane < fill[0, t], 1.0, 0.0)
        own[t, 7:8] = jnp.ones((1, N), F32)


def recall_body(states, held, mixed):
    def body(at):
        for n, (i, h, e) in enumerate(BLOCKS):
            one, two = (states[j, 0, h, first_offset(i) + e, at] for j in range(2))
            held[0, h, i, e, at] = one
            held[1, h, i, e, at] = two
            mixed[n, at] = 0.21 * one.astype(F32) + 0.2375 * two.astype(F32)

    each_chunk(body)


def measure(at, blocks, target, home, mixed, volume, swell, length_, lever_, weight_, pull_, rest_, stretch_):
    for n, (i, h, e) in enumerate(blocks):
        t = target(i, h, e)
        bond = [t[j : j + 1] - home[h][j] for j in range(3)]
        length = root(bond[0] * bond[0] + bond[1] * bond[1] + bond[2] * bond[2])
        close = jnp.maximum(t[6:7] - length, 0.0)
        weight = close * close
        gap = [t[3 + j : 4 + j] - home[h][3 + j] for j in range(3)]
        squared = gap[0] * gap[0] + gap[1] * gap[1] + gap[2] * gap[2]
        stretch = root(squared) - length
        lever = weight * length
        volume[h] = volume[h] + lever * length
        swell[h] = swell[h] + lever * stretch
        length_[n, at] = length
        lever_[n, at] = lever
        weight_[n, at] = weight
        pull_[n, at] = weight * lax.rsqrt(squared + 0.01)
        rest_[n, at] = 0.8475 * stretch - mixed[BLOCKS.index((i, h, e)), at]
        stretch_[n, at] = stretch


def inner_body(tiles, mixed, homes, volume_, swell_, *geo):
    for h in range(2):
        spread(homes, h, tiles[1, h], 7)

    def body(at):
        home = [[homes[h, j, at] for j in range(6)] for h in range(2)]
        volume = [jnp.zeros((CHUNK, N), F32)] * 2
        swell = [jnp.zeros((CHUNK, N), F32)] * 2
        measure(at, INNER, lambda i, h, e: tiles.at[i, h + e - 1], home, mixed, volume, swell, *geo)
        for h in range(2):
            volume_[h, at] = volume[h]
            swell_[h, at] = swell[h]

    each_chunk(body)


def press(which, force_of, place, homes, first_home, row_in, row_out, col_sum):
    col_sum[...] = jnp.zeros_like(col_sum)

    def body(at):
        for h in range(2):
            home = [homes[h, first_home + j, at] for j in range(3)]
            total = [jnp.zeros((CHUNK, N), F32) if row_in is None else row_in[3 * h + j, at] for j in range(3)]
            force = force_of(h, at)
            for n, i in enumerate(which):
                for e in range(3):
                    strength = force(i, e)
                    for j in range(3):
                        part = strength * (place(i, h, e, j) - home[j])
                        total[j] = total[j] + part
                        q = 128 * n + 32 * (h + e) + 8 * j
                        col_sum[q : q + 8] += part[0:8] + part[8:16]
            for j in range(3):
                row_out[3 * h + j, at] = total[j]

    each_chunk(body)


def by_other(col_sum, n):
    return -sum(col_sum[pl.ds(128 * n + k, 16, stride=8), :] for k in range(8))


def by_own(row_sum):
    lane = lax.broadcasted_iota(jnp.int32, (N, N), 1)
    table = jnp.zeros((N, N), F32)
    for h in range(2):
        for j in range(3):
            table = jnp.where(lane == 4 * h + 4 + j, jnp.sum(row_sum[3 * h + j], axis=1, keepdims=True), table)
    return jnp.transpose(table)[:16]


def first_forces(which, tiles, left, right, homes, shear, bulk, inner, outer, row_in, row_out, col_sum):
    def force_of(h, at):
        flat, tall = shear[h, at], bulk[h, at]

        def force(i, e):
            (length, pull, rest), n = either(inner, outer, i, h, e)
            return pull[n, at] * (length[n, at] * tall + rest[n, at] * flat)

        return force

    def place(i, h, e, j):
        return tile_of(tiles, left, right, i, h, e)[3 + j : 4 + j]

    press(which, force_of, place, homes, 3, row_in, row_out, col_sum)


def first_body(tiles, left, right, mixed, homes, volume_, swell_, *refs):
    inner, (push, third_, shear_, bulk, row_sum), refs = refs[:3], refs[3:8], refs[8:]
    outer, (vol, swl, col_sum) = refs[:6], refs[6:]

    def measure_outer(at):
        home = [[homes[h, j, at] for j in range(6)] for h in range(2)]
        volume = [volume_[h, at] for h in range(2)]
        swell = [swell_[h, at] for h in range(2)]
        measure(
            at, OUTER, lambda i, h, e: tile_of(tiles, left, right, i, h, e), home, mixed, volume, swell, *outer
        )
        for h in range(2):
            vol[h, at] = volume[h]
            swl[h, at] = swell[h]

    each_chunk(measure_outer)
    for h in range(2):
        here = homes[h, 6]
        mass = jnp.maximum(here * jnp.sum(vol[h], axis=1, keepdims=True), 1.0)
        share = here / mass
        dilatation = 3.0 * (share * jnp.sum(swl[h], axis=1, keepdims=True))
        shear = 7.5 * share
        third_[h] = dilatation / 3.0
        shear_[h] = shear
        bulk[h] = 0.1175 * dilatation * shear
    three = (outer[0], outer[3], outer[4])
    first_forces((0,), tiles, left, right, homes, shear_, bulk, inner, three, None, row_sum, col_sum)
    push[...] = 0.04 * by_other(col_sum, 0)


def first_rest_body(tiles, left, right, homes, state, shear, bulk, row_in, *refs):
    inner, outer, (push, row_sum, col_sum) = refs[:3], refs[3:6], refs[6:]
    first_forces((1, 2), tiles, left, right, homes, shear, bulk, inner, outer, row_in, row_sum, col_sum)
    push[0] = 0.04 * (by_own(row_sum) + by_other(col_sum, 0)) + state[0]
    push[1] = 0.04 * by_other(col_sum, 1)


def relax_body(held, third, shear, len_i, len_o, wgt_i, wgt_o, str_i, str_o, new, mixed, firm):
    def body(at):
        for h in range(2):
            lean, flat = third[h, at], shear[h, at]
            for i in range(3):
                for e in range(3):
                    (length, weight, stretch), n = either((len_i, wgt_i, str_i), (len_o, wgt_o, str_o), i, h, e)
                    m = BLOCKS.index((i, h, e))
                    deviator = stretch[n, at] - lean * length[n, at]
                    one = (0.6 * held[0, h, i, e, at].astype(F32) + 0.4 * deviator).astype(jnp.bfloat16)
                    two = (0.95 * held[1, h, i, e, at].astype(F32) + 0.05 * deviator).astype(jnp.bfloat16)
                    new[0, h, i, e, at] = one
                    new[1, h, i, e, at] = two
                    mixed[m, at] = 0.21 * one.astype(F32) + 0.2375 * two.astype(F32)
                    firm[m, at] = weight[n, at] * flat

    each_chunk(body)


def move(rows, tiles, left, right, pull, i, n):
    for c in range(4):
        t = tile_of(tiles, left, right, i, 0, c)
        rows[4 * n + c, 0:3] = t[0:3] + pull[4 * c : 4 * c + 3] * t[7:8]
        rows[4 * n + c, 3:8] = jnp.zeros((5, N), F32)


def stretches(which, rows, homes, swell_in, swell_out, mixed, firm, inner, outer, stretch_, kernel_, rest_):
    def body(at):
        for h in range(2):
            home = [homes[h, j, at] for j in range(3)]
            swell = jnp.zeros((CHUNK, N), F32) if swell_in is None else swell_in[h, at]
            for q, i in enumerate(which):
                for e in range(3):
                    (length, lever), n = either(inner, outer, i, h, e)
                    t, m, w = 4 * q + h + e, BLOCKS.index((i, h, e)), 6 * q + 3 * h + e
                    gap = [rows[t, j : j + 1] - home[j] for j in range(3)]
                    squared = gap[0] * gap[0] + gap[1] * gap[1] + gap[2] * gap[2]
                    stretch = root(squared) - length[n, at]
                    swell = swell + lever[n, at] * stretch
                    stretch_[w, at] = stretch
                    kernel_[w, at] = firm[m, at] * lax.rsqrt(squared + 0.01)
                    rest_[w, at] = 0.8475 * stretch - mixed[m, at]
            swell_out[h, at] = swell

    each_chunk(body)


def second_body(tiles, left, right, pull, state, mixed, firm, len_i, len_o, lev_i, lev_o, *refs):
    rows, homes, own, swell, stretch, kernel, rest = refs
    for n in range(2):
        move(rows, tiles, left, right, pull[n], 1 + n, n)
    own[0] = pull[0]
    own[1] = state[1] + 5.0 * (pull[0] - state[0])
    for h in range(2):
        spread(homes, h, rows[1 + h], 3)
    stretches((1, 2), rows, homes, None, swell, mixed, firm, (len_i, lev_i), (len_o, lev_o), stretch, kernel, rest)


def second_forces(which, rows, homes, bulk, inner, outer, geo, row_in, row_out, col_sum):
    def force_of(h, at):
        tall = bulk[h, at]

        def force(i, e):
            length, n = either(inner, outer, i, h, e)
            (kernel, rest), w = geo(i, h, e)
            return kernel[w, at] * (length[n, at] * tall + rest[w, at])

        return force

    def place(i, h, e, j):
        ref, n = rows(i)
        return ref[4 * n + h + e, j : j + 1]

    press(which, force_of, place, homes, 0, row_in, row_out, col_sum)


def second_side_body(
    tiles, left, right, pull, mixed, firm, len_i, len_o, lev_i, lev_o, shear, rows, homes, swell, kernel, rest, *refs
):
    push, third, bulk, row_sum, stretch_n, rows_n, swl, kernel_n, rest_n, col_sum = refs
    move(rows_n, tiles, left, right, pull, 0, 0)
    stretches(
        (0,), rows_n, homes, swell, swl, mixed, firm, (len_i, lev_i), (len_o, lev_o), stretch_n, kernel_n, rest_n
    )
    for h in range(2):
        dilatation = 0.4 * shear[h] * jnp.sum(swl[h], axis=1, keepdims=True)
        third[h] = dilatation / 3.0
        bulk[h] = 0.1175 * dilatation

    def geo(i, h, e):
        return ((kernel, rest), 6 + 3 * h + e) if i else ((kernel_n, rest_n), 3 * h + e)

    second_forces(
        (0, 2), lambda i: (rows, 1) if i else (rows_n, 0), homes, bulk, len_i, len_o, geo, None, row_sum, col_sum
    )
    for n in range(2):
        push[n] = by_other(col_sum, n)


def second_own_body(len_i, len_o, bulk, rows, homes, kernel, rest, row_in, push, row_sum, col_sum):
    def geo(i, h, e):
        return (kernel, rest), 3 * h + e

    second_forces((1,), lambda i: (rows, 0), homes, bulk, len_i, len_o, geo, row_in, row_sum, col_sum)
    push[...] = by_own(row_sum) + by_other(col_sum, 0)


def settle_body(held, third, len_i, len_o, stretch_n, stretch, new):
    def body(at):
        for h in range(2):
            lean = third[h, at]
            for i in range(3):
                for e in range(3):
                    length, n = either(len_i, len_o, i, h, e)
                    longer = stretch[6 * (i - 1) + 3 * h + e, at] if i else stretch_n[3 * h + e, at]
                    deviator = longer - lean * length[n, at]
                    one, two = held[0, h, i, e, at].astype(F32), held[1, h, i, e, at].astype(F32)
                    k = first_offset(i) + e
                    new[0, 0, h, k, at] = (0.6 * one + 0.4 * deviator).astype(jnp.bfloat16)
                    new[1, 0, h, k, at] = (0.95 * two + 0.05 * deviator).astype(jnp.bfloat16)

    each_chunk(body)


def finish_body(total, own, displacement, velocity):
    speed = own[1] + 0.2 * total[...]
    place = own[0] + 0.2 * speed
    for t in range(2):
        for j in range(3):
            q = 4 * (t + 1) + j
            velocity[j, 0, t : t + 1] = speed[q : q + 1]
            displacement[j, 0, t : t + 1] = place[q : q + 1]


def swap_pairs(size, parity):
    return [(i, (i + 1) % size if i % 2 == parity else (i - 1) % size) for i in range(size)]


def row_swaps(slabs, columns):
    pairs = []
    for s in range(slabs):
        for c in range(columns):
            if s in (0, slabs - 1):
                pairs.append((s * columns + c, s * columns + (c ^ 2)))
            else:
                pairs.append((s * columns + c, (s + 1 if s % 2 else s - 1) * columns + c))
    return pairs


def inner_swaps(slabs, columns):
    pairs = []
    for s in range(slabs):
        for c in range(columns):
            if c in (0, columns - 1):
                pairs.append((s * columns + c, (s ^ 1) * columns + c))
            else:
                pairs.append((s * columns + c, s * columns + (c + 1 if c % 2 else c - 1)))
    return pairs


def per_device(slabs, columns, rest_points, tile_fill, displacement, velocity, back_extension):
    s, c = lax.axis_index("slab"), lax.axis_index("col")
    c_odd, low, high = c % 2 == 1, c > 0, c < columns - 1
    inside = (s > 0) & (s < slabs - 1)
    c_odd, low, high, inside = lax.optimization_barrier((c_odd, low, high, inside))
    slab_near, slab_far = swap_pairs(slabs, 0), row_swaps(slabs, columns)
    col_near, col_far = swap_pairs(columns, 0), inner_swaps(slabs, columns)

    def to_near(values):
        return lax.ppermute(values, "slab", slab_near)

    def to_far(values):
        return lax.ppermute(values, ("slab", "col"), slab_far)

    def over_col(to_left, to_right):
        far = lax.ppermute(jnp.where(c_odd, to_right, to_left), ("slab", "col"), col_far)
        near = lax.ppermute(jnp.where(c_odd, to_left, to_right), "col", col_near)
        from_left = jnp.where(low, jnp.where(c_odd, near, far), 0.0)
        from_right = jnp.where(high, jnp.where(c_odd, far, near), 0.0)
        return from_left, from_right

    def add_over_col(sums):
        lo, hi = sums[..., :8, :], sums[..., 8:, :]
        from_left, from_right = over_col(lo, hi)
        return jnp.concatenate([lo + from_left, hi + from_right], axis=-2)

    history = jax.ShapeDtypeStruct((2, 2, 3, 3, N, N), back_extension.dtype)
    pages, big = block(2, N, N), block(6, N, N)
    column_sums = [pltpu.VMEM((128 * n, N), F32) for n in range(3)]
    row_sums = pltpu.VMEM((6, N, N), F32)
    hbm = pl.BlockSpec(memory_space=pl.ANY)
    own, state = call(
        pack_body,
        [block(2, 8, N), block(2, 16, N)],
        (tile_fill, rest_points, displacement, velocity),
        scratch=[pltpu.SMEM(tile_fill.shape, jnp.int32)]
        + [pltpu.VMEM(rest_points.shape, F32)] * 3
        + [pltpu.SemaphoreType.DMA((4,))],
        specs=[hbm] * 4,
        limit=None,
    )
    far = to_far(own)
    near = to_near(own)
    held, mixed = call(recall_body, [history, block(18, N, N)], (back_extension,), work=2_000_000)
    near, far, held, mixed = lax.optimization_barrier((near, far, held, mixed))
    tiles = jnp.stack([near, own, jnp.where(inside, far, 0.0)])
    left, right = over_col(tiles[:, 0], tiles[:, 1])
    homes, volume, swell, *inner = call(
        inner_body, [block(2, 7, N, N), pages, pages] + [block(12, N, N)] * 6, (tiles, mixed), work=6_000_000
    )
    three_i = (inner[0], inner[3], inner[4])
    push, third, shear, bulk, rows, *outer = call(
        first_body,
        [block(16, N), pages, pages, pages, big] + [big] * 6,
        (tiles, left, right, mixed, homes, volume, swell, *three_i),
        scratch=[pltpu.VMEM((2, N, N), F32)] * 2 + [column_sums[1]],
        work=4_000_000,
    )
    got = to_near(push)
    (push,) = call(
        first_rest_body,
        [block(2, 16, N)],
        (tiles, left, right, homes, state, shear, bulk, rows, *three_i, outer[0], outer[3], outer[4]),
        scratch=[row_sums, column_sums[2]],
        work=4_000_000,
    )
    got, push = lax.optimization_barrier((got, push))
    two = jnp.stack([push[0] + got, push[1]])
    back = to_far(two)
    held, mixed, firm = call(
        relax_body,
        [history, block(18, N, N), block(18, N, N)],
        (held, third, shear, inner[0], outer[0], inner[2], outer[2], inner[5], outer[5]),
        work=4_000_000,
    )
    back, held, mixed, firm = lax.optimization_barrier((back, held, mixed, firm))
    back = jnp.where(inside, back, 0.0)
    pull = add_over_col(two + jnp.stack([back[1], back[0]]))
    pull_near = to_near(pull[0])
    geometry = (mixed, firm, inner[0], outer[0], inner[1], outer[1])
    moved, homes, state, swell, stretch, kernel, rest = call(
        second_body,
        [block(8, 8, N), block(2, 3, N, N), block(2, 16, N), pages] + [block(12, N, N)] * 3,
        (tiles, left, right, pull, state, *geometry),
        work=4_000_000,
    )
    pull_near, swell = lax.optimization_barrier((pull_near, swell))
    push, third, bulk, rows, stretch_near = call(
        second_side_body,
        [block(2, 16, N), pages, pages, big, big],
        (tiles, left, right, pull_near, *geometry, shear, moved, homes, swell, kernel, rest),
        scratch=[pltpu.VMEM((4, 8, N), F32), pltpu.VMEM((2, N, N), F32), row_sums, row_sums, column_sums[2]],
        work=4_000_000,
    )
    far = to_far(push[1])
    near = to_near(push[0])
    (push,) = call(
        second_own_body,
        [block(16, N)],
        (inner[0], outer[0], bulk, moved, homes, kernel, rest, rows),
        scratch=[row_sums, column_sums[1]],
        work=4_000_000,
    )
    near, far, push = lax.optimization_barrier((near, far, push))
    total = add_over_col(push + near + jnp.where(inside, far, 0.0))
    (held,) = call(
        settle_body,
        [jax.ShapeDtypeStruct(back_extension.shape, back_extension.dtype)],
        (held, third, inner[0], outer[0], stretch_near, stretch),
        work=3_000_000,
    )
    shape = block(*rest_points.shape)
    displacement, velocity = call(finish_body, [shape, shape], (total, state))
    return (displacement, velocity, held)


def solution(mesh):
    in_specs = (
        P(None, "slab", "col", None),
        P("slab", "col"),
        P(None, "slab", "col", None),
        P(None, "slab", "col", None),
        P(None, "slab", "col", None, None, None),
    )
    out_specs = (
        P(None, "slab", "col", None),
        P(None, "slab", "col", None),
        P(None, "slab", "col", None, None, None),
    )
    return jax.shard_map(
        functools.partial(per_device, mesh.shape["slab"], mesh.shape["col"]),
        mesh=mesh,
        in_specs=in_specs,
        out_specs=out_specs,
        check_vma=False,
    )
```

```python
import functools

import jax
import jax.numpy as jnp
from jax import lax
from jax.experimental import pallas as pl
from jax.experimental.pallas import tpu as pltpu
from jax.sharding import PartitionSpec as P


N = 128
CHUNK = 16
F32 = jnp.float32
VMEM = pl.BlockSpec(memory_space=pltpu.VMEM)
BLOCKS = [(i, h, e) for i in range(3) for h in range(2) for e in range(3)]
INNER = [b for b in BLOCKS if 1 <= b[1] + b[2] <= 2]
OUTER = [b for b in BLOCKS if not 1 <= b[1] + b[2] <= 2]


def root(squared):
    return squared * lax.rsqrt(jnp.maximum(squared, 1e-36))


def block(*shape):
    return jax.ShapeDtypeStruct(shape, F32)


def call(body, outs, operands, scratch=(), specs=None, work=0, limit=24):
    cost = pl.CostEstimate(flops=work, bytes_accessed=1 << 16, transcendentals=0) if work else None
    return pl.pallas_call(
        body,
        out_shape=outs,
        in_specs=specs or [VMEM] * len(operands),
        out_specs=[VMEM] * len(outs),
        scratch_shapes=list(scratch),
        compiler_params=pltpu.CompilerParams(vmem_limit_bytes=limit and limit * 1024 * 1024),
        cost_estimate=cost,
    )(*operands)


def each_chunk(body):
    def step(i, carry):
        body(pl.ds(pl.multiple_of(i * CHUNK, CHUNK), CHUNK))
        return carry

    lax.fori_loop(0, N // CHUNK, step, 0)


def first_offset(i):
    odd = lax.axis_index("slab") % 2
    return (6 * (1 - odd), 3, 6 * odd)[i]


def spread(homes, h, tile, count):
    columns = jnp.transpose(tile)
    for j in range(count):
        homes[h, j] = jnp.broadcast_to(columns[:, j : j + 1], (N, N))


def either(inner, outer, i, h, e):
    if (i, h, e) in INNER:
        return inner, INNER.index((i, h, e))
    return outer, OUTER.index((i, h, e))


def tile_of(tiles, left, right, i, h, e):
    c = h + e
    return tiles.at[i, c - 1] if c in (1, 2) else (right if c else left).at[i]


def pack_body(fill_far, rest_far, shift_far, own, fill, rest, shift, sems):
    pairs = ((fill_far, fill), (rest_far, rest), (shift_far, shift))
    copies = [pltpu.make_async_copy(a, b, sems.at[i]) for i, (a, b) in enumerate(pairs)]
    for copy in copies:
        copy.start()
    for copy in copies:
        copy.wait()
    lane = lax.broadcasted_iota(jnp.int32, (1, N), 1)
    for t in range(2):
        for j in range(3):
            own[t, j : j + 1] = rest[j, 0, t : t + 1]
            own[t, 3 + j : 4 + j] = rest[j, 0, t : t + 1] + shift[j, 0, t : t + 1]
        own[t, 6:7] = jnp.where(lane < fill[0, t], 1.0, 0.0)
        own[t, 7:8] = jnp.ones((1, N), F32)


def recall_body(states, held, mixed):
    def body(at):
        for n, (i, h, e) in enumerate(BLOCKS):
            one, two = (states[j, 0, h, first_offset(i) + e, at] for j in range(2))
            held[0, h, i, e, at] = one
            held[1, h, i, e, at] = two
            mixed[n, at] = 0.21 * one.astype(F32) + 0.2375 * two.astype(F32)

    each_chunk(body)


def measure(at, blocks, target, home, mixed, volume, swell, length_, lever_, weight_, pull_, rest_, stretch_):
    for n, (i, h, e) in enumerate(blocks):
        t = target(i, h, e)
        bond = [t[j : j + 1] - home[h][j] for j in range(3)]
        length = root(bond[0] * bond[0] + bond[1] * bond[1] + bond[2] * bond[2])
        close = jnp.maximum(t[6:7] - length, 0.0)
        weight = close * close
        gap = [t[3 + j : 4 + j] - home[h][3 + j] for j in range(3)]
        squared = gap[0] * gap[0] + gap[1] * gap[1] + gap[2] * gap[2]
        stretch = root(squared) - length
        lever = weight * length
        volume[h] = volume[h] + lever * length
        swell[h] = swell[h] + lever * stretch
        length_[n, at] = length
        lever_[n, at] = lever
        weight_[n, at] = weight
        pull_[n, at] = weight * lax.rsqrt(squared + 0.01)
        rest_[n, at] = 0.8475 * stretch - mixed[BLOCKS.index((i, h, e)), at]
        stretch_[n, at] = stretch


def inner_body(tiles, mixed, homes, volume_, swell_, *geo):
    for h in range(2):
        spread(homes, h, tiles[1, h], 7)

    def body(at):
        home = [[homes[h, j, at] for j in range(6)] for h in range(2)]
        volume = [jnp.zeros((CHUNK, N), F32)] * 2
        swell = [jnp.zeros((CHUNK, N), F32)] * 2
        measure(at, INNER, lambda i, h, e: tiles.at[i, h + e - 1], home, mixed, volume, swell, *geo)
        for h in range(2):
            volume_[h, at] = volume[h]
            swell_[h, at] = swell[h]

    each_chunk(body)


def press(which, force_of, place, homes, first_home, row_in, row_out, col_sum):
    col_sum[...] = jnp.zeros_like(col_sum)

    def body(at):
        for h in range(2):
            home = [homes[h, first_home + j, at] for j in range(3)]
            total = [jnp.zeros((CHUNK, N), F32) if row_in is None else row_in[3 * h + j, at] for j in range(3)]
            force = force_of(h, at)
            for n, i in enumerate(which):
                for e in range(3):
                    strength = force(i, e)
                    for j in range(3):
                        part = strength * (place(i, h, e, j) - home[j])
                        total[j] = total[j] + part
                        q = 128 * n + 32 * (h + e) + 8 * j
                        col_sum[q : q + 8] += part[0:8] + part[8:16]
            for j in range(3):
                row_out[3 * h + j, at] = total[j]

    each_chunk(body)


def by_other(col_sum, n):
    return -sum(col_sum[pl.ds(128 * n + k, 16, stride=8), :] for k in range(8))


def by_own(row_sum):
    lane = lax.broadcasted_iota(jnp.int32, (N, N), 1)
    table = jnp.zeros((N, N), F32)
    for h in range(2):
        for j in range(3):
            table = jnp.where(lane == 4 * h + 4 + j, jnp.sum(row_sum[3 * h + j], axis=1, keepdims=True), table)
    return jnp.transpose(table)[:16]


def first_forces(which, tiles, left, right, homes, shear, bulk, inner, outer, row_in, row_out, col_sum):
    def force_of(h, at):
        flat, tall = shear[h, at], bulk[h, at]

        def force(i, e):
            (length, pull, rest), n = either(inner, outer, i, h, e)
            return pull[n, at] * (length[n, at] * tall + rest[n, at] * flat)

        return force

    def place(i, h, e, j):
        return tile_of(tiles, left, right, i, h, e)[3 + j : 4 + j]

    press(which, force_of, place, homes, 3, row_in, row_out, col_sum)


def first_body(tiles, left, right, mixed, homes, volume_, swell_, *refs):
    inner, (push, third_, shear_, bulk, row_sum), refs = refs[:3], refs[3:8], refs[8:]
    outer, (vol, swl, col_sum) = refs[:6], refs[6:]

    def measure_outer(at):
        home = [[homes[h, j, at] for j in range(6)] for h in range(2)]
        volume = [volume_[h, at] for h in range(2)]
        swell = [swell_[h, at] for h in range(2)]
        measure(
            at, OUTER, lambda i, h, e: tile_of(tiles, left, right, i, h, e), home, mixed, volume, swell, *outer
        )
        for h in range(2):
            vol[h, at] = volume[h]
            swl[h, at] = swell[h]

    each_chunk(measure_outer)
    for h in range(2):
        here = homes[h, 6]
        mass = jnp.maximum(here * jnp.sum(vol[h], axis=1, keepdims=True), 1.0)
        share = here / mass
        dilatation = 3.0 * (share * jnp.sum(swl[h], axis=1, keepdims=True))
        shear = 7.5 * share
        third_[h] = dilatation / 3.0
        shear_[h] = shear
        bulk[h] = 0.1175 * dilatation * shear
    three = (outer[0], outer[3], outer[4])
    first_forces((0,), tiles, left, right, homes, shear_, bulk, inner, three, None, row_sum, col_sum)
    push[...] = 0.04 * by_other(col_sum, 0)


def first_rest_body(tiles, left, right, homes, shift, speed, shear, bulk, row_in, *refs):
    inner, outer, (push, state, row_sum, col_sum) = refs[:3], refs[3:6], refs[6:]
    state[...] = jnp.zeros_like(state)
    for h in range(2):
        for j in range(3):
            q = 4 * h + 4 + j
            state[0, q : q + 1] = shift[j, 0, h : h + 1] + 0.2 * speed[j, 0, h : h + 1]
            state[1, q : q + 1] = speed[j, 0, h : h + 1]
    first_forces((1, 2), tiles, left, right, homes, shear, bulk, inner, outer, row_in, row_sum, col_sum)
    push[0] = 0.04 * (by_own(row_sum) + by_other(col_sum, 0)) + state[0]
    push[1] = 0.04 * by_other(col_sum, 1)


def relax_body(held, third, shear, len_i, len_o, wgt_i, wgt_o, str_i, str_o, new, mixed, firm):
    def body(at):
        for h in range(2):
            lean, flat = third[h, at], shear[h, at]
            for i in range(3):
                for e in range(3):
                    (length, weight, stretch), n = either((len_i, wgt_i, str_i), (len_o, wgt_o, str_o), i, h, e)
                    m = BLOCKS.index((i, h, e))
                    deviator = stretch[n, at] - lean * length[n, at]
                    one = (0.6 * held[0, h, i, e, at].astype(F32) + 0.4 * deviator).astype(jnp.bfloat16)
                    two = (0.95 * held[1, h, i, e, at].astype(F32) + 0.05 * deviator).astype(jnp.bfloat16)
                    new[0, h, i, e, at] = one
                    new[1, h, i, e, at] = two
                    mixed[m, at] = 0.21 * one.astype(F32) + 0.2375 * two.astype(F32)
                    firm[m, at] = weight[n, at] * flat

    each_chunk(body)


def move(rows, tiles, left, right, pull, i, n):
    for c in range(4):
        t = tile_of(tiles, left, right, i, 0, c)
        rows[4 * n + c, 0:3] = t[0:3] + pull[4 * c : 4 * c + 3] * t[7:8]
        rows[4 * n + c, 3:8] = jnp.zeros((5, N), F32)


def stretches(which, rows, homes, swell_in, swell_out, mixed, firm, inner, outer, stretch_, kernel_, rest_):
    def body(at):
        for h in range(2):
            home = [homes[h, j, at] for j in range(3)]
            swell = jnp.zeros((CHUNK, N), F32) if swell_in is None else swell_in[h, at]
            for q, i in enumerate(which):
                for e in range(3):
                    (length, lever), n = either(inner, outer, i, h, e)
                    t, m, w = 4 * q + h + e, BLOCKS.index((i, h, e)), 6 * q + 3 * h + e
                    gap = [rows[t, j : j + 1] - home[j] for j in range(3)]
                    squared = gap[0] * gap[0] + gap[1] * gap[1] + gap[2] * gap[2]
                    stretch = root(squared) - length[n, at]
                    swell = swell + lever[n, at] * stretch
                    stretch_[w, at] = stretch
                    kernel_[w, at] = firm[m, at] * lax.rsqrt(squared + 0.01)
                    rest_[w, at] = 0.8475 * stretch - mixed[m, at]
            swell_out[h, at] = swell

    each_chunk(body)


def second_body(tiles, left, right, pull, state, mixed, firm, len_i, len_o, lev_i, lev_o, *refs):
    rows, homes, own, swell, stretch, kernel, rest = refs
    for n in range(2):
        move(rows, tiles, left, right, pull[n], 1 + n, n)
    own[0] = pull[0]
    own[1] = state[1] + 5.0 * (pull[0] - state[0])
    for h in range(2):
        spread(homes, h, rows[1 + h], 3)
    stretches((1, 2), rows, homes, None, swell, mixed, firm, (len_i, lev_i), (len_o, lev_o), stretch, kernel, rest)


def second_forces(which, rows, homes, bulk, inner, outer, geo, row_in, row_out, col_sum):
    def force_of(h, at):
        tall = bulk[h, at]

        def force(i, e):
            length, n = either(inner, outer, i, h, e)
            (kernel, rest), w = geo(i, h, e)
            return kernel[w, at] * (length[n, at] * tall + rest[w, at])

        return force

    def place(i, h, e, j):
        ref, n = rows(i)
        return ref[4 * n + h + e, j : j + 1]

    press(which, force_of, place, homes, 0, row_in, row_out, col_sum)


def second_side_body(
    tiles, left, right, pull, mixed, firm, len_i, len_o, lev_i, lev_o, shear, rows, homes, swell, kernel, rest, *refs
):
    push, third, bulk, row_sum, stretch_n, rows_n, kernel_n, rest_n, swl, col_sum = refs
    move(rows_n, tiles, left, right, pull, 0, 0)
    stretches(
        (0,), rows_n, homes, swell, swl, mixed, firm, (len_i, lev_i), (len_o, lev_o), stretch_n, kernel_n, rest_n
    )
    for h in range(2):
        dilatation = 0.4 * shear[h] * jnp.sum(swl[h], axis=1, keepdims=True)
        third[h] = dilatation / 3.0
        bulk[h] = 0.1175 * dilatation

    def geo(i, h, e):
        return (kernel, rest), 6 + 3 * h + e

    second_forces((2,), lambda i: (rows, 1), homes, bulk, len_i, len_o, geo, None, row_sum, col_sum)
    push[...] = by_other(col_sum, 0)


def second_own_body(
    len_i, len_o, bulk, rows, rows_n, homes, kernel, rest, kernel_n, rest_n, row_in, push, row_sum, col_sum
):
    def geo(i, h, e):
        return ((kernel, rest) if i else (kernel_n, rest_n)), 3 * h + e

    second_forces(
        (0, 1), lambda i: (rows if i else rows_n, 0), homes, bulk, len_i, len_o, geo, row_in, row_sum, col_sum
    )
    push[0] = by_other(col_sum, 0)
    push[1] = by_own(row_sum) + by_other(col_sum, 1)


def settle_body(held, third, len_i, len_o, stretch_n, stretch, new):
    def body(at):
        for h in range(2):
            lean = third[h, at]
            for i in range(3):
                for e in range(3):
                    length, n = either(len_i, len_o, i, h, e)
                    longer = stretch[6 * (i - 1) + 3 * h + e, at] if i else stretch_n[3 * h + e, at]
                    deviator = longer - lean * length[n, at]
                    one, two = held[0, h, i, e, at].astype(F32), held[1, h, i, e, at].astype(F32)
                    k = first_offset(i) + e
                    new[0, 0, h, k, at] = (0.6 * one + 0.4 * deviator).astype(jnp.bfloat16)
                    new[1, 0, h, k, at] = (0.95 * two + 0.05 * deviator).astype(jnp.bfloat16)

    each_chunk(body)


def finish_body(total, own, displacement, velocity):
    speed = own[1] + 0.2 * total[...]
    place = own[0] + 0.2 * speed
    for t in range(2):
        for j in range(3):
            q = 4 * (t + 1) + j
            velocity[j, 0, t : t + 1] = speed[q : q + 1]
            displacement[j, 0, t : t + 1] = place[q : q + 1]


def swap_pairs(size, parity):
    return [(i, (i + 1) % size if i % 2 == parity else (i - 1) % size) for i in range(size)]


def row_swaps(slabs, columns):
    pairs = []
    for s in range(slabs):
        for c in range(columns):
            if s in (0, slabs - 1):
                pairs.append((s * columns + c, s * columns + (c ^ 2)))
            else:
                pairs.append((s * columns + c, (s + 1 if s % 2 else s - 1) * columns + c))
    return pairs


def inner_swaps(slabs, columns):
    pairs = []
    for s in range(slabs):
        for c in range(columns):
            if c in (0, columns - 1):
                pairs.append((s * columns + c, (s ^ 1) * columns + c))
            else:
                pairs.append((s * columns + c, s * columns + (c + 1 if c % 2 else c - 1)))
    return pairs


def per_device(slabs, columns, rest_points, tile_fill, displacement, velocity, back_extension):
    s, c = lax.axis_index("slab"), lax.axis_index("col")
    c_odd, low, high = c % 2 == 1, c > 0, c < columns - 1
    inside = (s > 0) & (s < slabs - 1)
    c_odd, low, high, inside = lax.optimization_barrier((c_odd, low, high, inside))
    slab_near, slab_far = swap_pairs(slabs, 0), row_swaps(slabs, columns)
    col_near, col_far = swap_pairs(columns, 0), inner_swaps(slabs, columns)

    def to_near(values):
        return lax.ppermute(values, "slab", slab_near)

    def to_far(values):
        return lax.ppermute(values, ("slab", "col"), slab_far)

    def over_col(to_left, to_right):
        far = lax.ppermute(jnp.where(c_odd, to_right, to_left), ("slab", "col"), col_far)
        near = lax.ppermute(jnp.where(c_odd, to_left, to_right), "col", col_near)
        from_left = jnp.where(low, jnp.where(c_odd, near, far), 0.0)
        from_right = jnp.where(high, jnp.where(c_odd, far, near), 0.0)
        return from_left, from_right

    def add_over_col(sums):
        lo, hi = sums[..., :8, :], sums[..., 8:, :]
        from_left, from_right = over_col(lo, hi)
        return jnp.concatenate([lo + from_left, hi + from_right], axis=-2)

    history = jax.ShapeDtypeStruct((2, 2, 3, 3, N, N), back_extension.dtype)
    pages, big = block(2, N, N), block(6, N, N)
    column_sums = [pltpu.VMEM((128 * n, N), F32) for n in range(3)]
    row_sums = pltpu.VMEM((6, N, N), F32)
    hbm = pl.BlockSpec(memory_space=pl.ANY)
    (own,) = call(
        pack_body,
        [block(2, 8, N)],
        (tile_fill, rest_points, displacement),
        scratch=[pltpu.SMEM(tile_fill.shape, jnp.int32)]
        + [pltpu.VMEM(rest_points.shape, F32)] * 2
        + [pltpu.SemaphoreType.DMA((3,))],
        specs=[hbm] * 3,
        limit=None,
    )
    far = to_far(own)
    near = to_near(own)
    held, mixed = call(recall_body, [history, block(18, N, N)], (back_extension,), work=2_000_000)
    near, far, held, mixed = lax.optimization_barrier((near, far, held, mixed))
    tiles = jnp.stack([near, own, jnp.where(inside, far, 0.0)])
    left, right = over_col(tiles[:, 0], tiles[:, 1])
    homes, volume, swell, *inner = call(
        inner_body, [block(2, 7, N, N), pages, pages] + [block(12, N, N)] * 6, (tiles, mixed), work=6_000_000
    )
    three_i = (inner[0], inner[3], inner[4])
    push, third, shear, bulk, rows, *outer = call(
        first_body,
        [block(16, N), pages, pages, pages, big] + [big] * 6,
        (tiles, left, right, mixed, homes, volume, swell, *three_i),
        scratch=[pltpu.VMEM((2, N, N), F32)] * 2 + [column_sums[1]],
        work=4_000_000,
    )
    got = to_near(push)
    push, state = call(
        first_rest_body,
        [block(2, 16, N), block(2, 16, N)],
        (tiles, left, right, homes, displacement, velocity, shear, bulk, rows, *three_i, outer[0], outer[3], outer[4]),
        scratch=[row_sums, column_sums[2]],
        work=4_000_000,
    )
    got, push = lax.optimization_barrier((got, push))
    two = jnp.stack([push[0] + got, push[1]])
    back = to_far(two)
    held, mixed, firm = call(
        relax_body,
        [history, block(18, N, N), block(18, N, N)],
        (held, third, shear, inner[0], outer[0], inner[2], outer[2], inner[5], outer[5]),
        work=4_000_000,
    )
    back, held, mixed, firm = lax.optimization_barrier((back, held, mixed, firm))
    back = jnp.where(inside, back, 0.0)
    pull = add_over_col(two + jnp.stack([back[1], back[0]]))
    pull_near = to_near(pull[0])
    geometry = (mixed, firm, inner[0], outer[0], inner[1], outer[1])
    moved, homes, state, swell, stretch, kernel, rest = call(
        second_body,
        [block(8, 8, N), block(2, 3, N, N), block(2, 16, N), pages] + [block(12, N, N)] * 3,
        (tiles, left, right, pull, state, *geometry),
        work=4_000_000,
    )
    pull_near, swell = lax.optimization_barrier((pull_near, swell))
    push, third, bulk, rows, stretch_near, moved_near, kernel_near, rest_near = call(
        second_side_body,
        [block(16, N), pages, pages, big, big, block(4, 8, N), big, big],
        (tiles, left, right, pull_near, *geometry, shear, moved, homes, swell, kernel, rest),
        scratch=[pltpu.VMEM((2, N, N), F32), column_sums[1]],
        work=4_000_000,
    )
    far = to_far(push)
    (push,) = call(
        second_own_body,
        [block(2, 16, N)],
        (inner[0], outer[0], bulk, moved, moved_near, homes, kernel, rest, kernel_near, rest_near, rows),
        scratch=[row_sums, column_sums[2]],
        work=4_000_000,
    )
    near = to_near(push[0])
    near, far, push = lax.optimization_barrier((near, far, push[1]))
    total = add_over_col(push + near + jnp.where(inside, far, 0.0))
    (held,) = call(
        settle_body,
        [jax.ShapeDtypeStruct(back_extension.shape, back_extension.dtype)],
        (held, third, inner[0], outer[0], stretch_near, stretch),
        work=3_000_000,
    )
    shape = block(*rest_points.shape)
    displacement, velocity = call(finish_body, [shape, shape], (total, state))
    return (displacement, velocity, held)


def solution(mesh):
    in_specs = (
        P(None, "slab", "col", None),
        P("slab", "col"),
        P(None, "slab", "col", None),
        P(None, "slab", "col", None),
        P(None, "slab", "col", None, None, None),
    )
    out_specs = (
        P(None, "slab", "col", None),
        P(None, "slab", "col", None),
        P(None, "slab", "col", None, None, None),
    )
    return jax.shard_map(
        functools.partial(per_device, mesh.shape["slab"], mesh.shape["col"]),
        mesh=mesh,
        in_specs=in_specs,
        out_specs=out_specs,
        check_vma=False,
    )
```

```python
import functools

import jax
import jax.numpy as jnp
from jax import lax
from jax.experimental import pallas as pl
from jax.experimental.pallas import tpu as pltpu
from jax.sharding import PartitionSpec as P


N = 128
CHUNK = 32
F32 = jnp.float32
VMEM = pl.BlockSpec(memory_space=pltpu.VMEM)
BLOCKS = [(i, h, e) for i in range(3) for h in range(2) for e in range(3)]
INNER = [b for b in BLOCKS if 1 <= b[1] + b[2] <= 2]
OUTER = [b for b in BLOCKS if not 1 <= b[1] + b[2] <= 2]


def root(squared):
    return squared * lax.rsqrt(jnp.maximum(squared, 1e-36))


def block(*shape):
    return jax.ShapeDtypeStruct(shape, F32)


def call(body, outs, operands, scratch=(), specs=None, work=0, limit=24, aliases=None):
    cost = pl.CostEstimate(flops=work, bytes_accessed=1 << 16, transcendentals=0) if work else None
    return pl.pallas_call(
        body,
        out_shape=outs,
        in_specs=specs or [VMEM] * len(operands),
        out_specs=[VMEM] * len(outs),
        scratch_shapes=list(scratch),
        compiler_params=pltpu.CompilerParams(vmem_limit_bytes=limit and limit * 1024 * 1024),
        cost_estimate=cost,
        input_output_aliases=aliases or {},
    )(*operands)


def each_chunk(body):
    def step(i, carry):
        body(pl.ds(pl.multiple_of(i * CHUNK, CHUNK), CHUNK))
        return carry

    lax.fori_loop(0, N // CHUNK, step, 0, unroll=2)


def first_offset(i):
    odd = lax.axis_index("slab") % 2
    return (6 * (1 - odd), 3, 6 * odd)[i]


def spread(homes, h, tile, count):
    columns = jnp.transpose(tile)
    for j in range(count):
        homes[h, j] = jnp.broadcast_to(columns[:, j : j + 1], (N, N))


def either(inner, outer, i, h, e):
    if (i, h, e) in INNER:
        return inner, INNER.index((i, h, e))
    return outer, OUTER.index((i, h, e))


def tile_of(tiles, left, right, i, h, e):
    c = h + e
    return tiles.at[i, c - 1] if c in (1, 2) else (right if c else left).at[i]


def pack_body(fill_far, rest_far, shift_far, own, fill, rest, shift, sems):
    pairs = ((fill_far, fill), (rest_far, rest), (shift_far, shift))
    copies = [pltpu.make_async_copy(a, b, sems.at[i]) for i, (a, b) in enumerate(pairs)]
    for copy in copies:
        copy.start()
    for copy in copies:
        copy.wait()
    lane = lax.broadcasted_iota(jnp.int32, (1, N), 1)
    for t in range(2):
        for j in range(3):
            own[t, j : j + 1] = rest[j, 0, t : t + 1]
            own[t, 3 + j : 4 + j] = rest[j, 0, t : t + 1] + shift[j, 0, t : t + 1]
        own[t, 6:7] = jnp.where(lane < fill[0, t], 1.0, 0.0)
        own[t, 7:8] = jnp.ones((1, N), F32)


def recall_body(states, held, mixed):
    def body(at):
        for n, (i, h, e) in enumerate(BLOCKS):
            one, two = (states[j, 0, h, first_offset(i) + e, at] for j in range(2))
            held[0, h, i, e, at] = one
            held[1, h, i, e, at] = two
            mixed[n, at] = 0.21 * one.astype(F32) + 0.2375 * two.astype(F32)

    each_chunk(body)


def measure(at, items, home, mixed, volume, swell, length_, lever_, weight_, pull_, rest_, stretch_):
    for t, h, n, m in items:
        bond = [t[j : j + 1] - home[h][j] for j in range(3)]
        length = root(bond[0] * bond[0] + bond[1] * bond[1] + bond[2] * bond[2])
        close = jnp.maximum(t[6:7] - length, 0.0)
        weight = close * close
        gap = [t[3 + j : 4 + j] - home[h][3 + j] for j in range(3)]
        squared = gap[0] * gap[0] + gap[1] * gap[1] + gap[2] * gap[2]
        stretch = root(squared) - length
        lever = weight * length
        volume[h] = volume[h] + lever * length
        swell[h] = swell[h] + lever * stretch
        length_[n, at] = length
        lever_[n, at] = lever
        weight_[n, at] = weight
        pull_[n, at] = weight * lax.rsqrt(squared + 0.01)
        rest_[n, at] = 0.8475 * stretch - mixed[m, at]
        stretch_[n, at] = stretch


def inner_body(tiles, mixed, homes, volume_, swell_, *geo):
    for h in range(2):
        spread(homes, h, tiles[1, h], 7)

    def body(at):
        home = [[homes[h, j, at] for j in range(6)] for h in range(2)]
        volume = [jnp.zeros((CHUNK, N), F32)] * 2
        swell = [jnp.zeros((CHUNK, N), F32)] * 2
        items = [(tiles.at[i, h + e - 1], h, n, BLOCKS.index((i, h, e))) for n, (i, h, e) in enumerate(INNER)]
        measure(at, items, home, mixed, volume, swell, *geo)
        for h in range(2):
            volume_[h, at] = volume[h]
            swell_[h, at] = swell[h]

    each_chunk(body)


def measure_side(h, ghost, mixed, homes, volume_in, swell_in, volume_out, swell_out, geo):
    def body(at):
        volume, swell = [volume_in[h, at]], [swell_in[h, at]]
        home = [[homes[h, j, at] for j in range(6)]]
        items = [(ghost.at[i], 0, 2 * i + h, 6 * i + 5 * h) for i in range(3)]
        measure(at, items, home, mixed, volume, swell, *geo)
        volume_out[h, at] = volume[0]
        swell_out[h, at] = swell[0]
        volume_out[1 - h, at] = volume_in[1 - h, at]
        swell_out[1 - h, at] = swell_in[1 - h, at]

    each_chunk(body)


def outer_body(columns, arrived, mixed, homes, volume_in, swell_in, volume_out, swell_out, *refs):
    geo, ghost = refs[:6], refs[6]
    c = lax.axis_index("col")
    ghost[...] = jnp.where((c > 0) & (c < columns - 1), arrived[...], 0.0)
    measure_side(c % 2, ghost, mixed, homes, volume_in, swell_in, volume_out, swell_out, geo)


def press(which, force_of, place, homes, first_home, row_in, row_out, col_sum):
    col_sum[...] = jnp.zeros_like(col_sum)

    def body(at):
        for h in range(2):
            home = [homes[h, first_home + j, at] for j in range(3)]
            total = [jnp.zeros((CHUNK, N), F32) if row_in is None else row_in[3 * h + j, at] for j in range(3)]
            force = force_of(h, at)
            for n, i in enumerate(which):
                for e in range(3):
                    strength = force(i, e)
                    for j in range(3):
                        part = strength * (place(i, h, e, j) - home[j])
                        total[j] = total[j] + part
                        q = 128 * n + 32 * (h + e) + 8 * j
                        col_sum[q : q + 8] += (part[0:8] + part[8:16]) + (part[16:24] + part[24:32])
            for j in range(3):
                row_out[3 * h + j, at] = total[j]

    each_chunk(body)


def by_other(col_sum, n):
    return -sum(col_sum[pl.ds(128 * n + k, 16, stride=8), :] for k in range(8))


def by_own(row_sum):
    lane = lax.broadcasted_iota(jnp.int32, (N, N), 1)
    table = jnp.zeros((N, N), F32)
    for h in range(2):
        for j in range(3):
            table = jnp.where(lane == 4 * h + 4 + j, jnp.sum(row_sum[3 * h + j], axis=1, keepdims=True), table)
    return jnp.transpose(table)[:16]


def first_forces(which, tiles, left, right, homes, shear, bulk, inner, outer, row_in, row_out, col_sum):
    def force_of(h, at):
        flat, tall = shear[h, at], bulk[h, at]

        def force(i, e):
            (length, pull, rest), n = either(inner, outer, i, h, e)
            return pull[n, at] * (length[n, at] * tall + rest[n, at] * flat)

        return force

    def place(i, h, e, j):
        return tile_of(tiles, left, right, i, h, e)[3 + j : 4 + j]

    press(which, force_of, place, homes, 3, row_in, row_out, col_sum)


def first_body(tiles, left, right, ghost, mixed, homes, volume_, swell_, *refs):
    inner, (push, third_, shear_, bulk, row_sum), refs = refs[:3], refs[9:14], refs[14:]
    outer, (vol, swl, col_sum) = refs[:6], refs[6:]
    near = 1 - lax.axis_index("col") % 2
    measure_side(near, ghost, mixed, homes, volume_, swell_, vol, swl, outer)
    for h in range(2):
        here = homes[h, 6]
        mass = jnp.maximum(here * jnp.sum(vol[h], axis=1, keepdims=True), 1.0)
        share = here / mass
        dilatation = 3.0 * (share * jnp.sum(swl[h], axis=1, keepdims=True))
        shear = 7.5 * share
        third_[h] = dilatation / 3.0
        shear_[h] = shear
        bulk[h] = 0.1175 * dilatation * shear
    three = (outer[0], outer[3], outer[4])
    first_forces((0,), tiles, left, right, homes, shear_, bulk, inner, three, None, row_sum, col_sum)
    push[...] = 0.04 * by_other(col_sum, 0)


def first_rest_body(tiles, left, right, homes, shift, speed, shear, bulk, row_in, *refs):
    inner, outer, (push, state, row_sum, col_sum) = refs[:3], refs[3:6], refs[6:]
    state[...] = jnp.zeros_like(state)
    for h in range(2):
        for j in range(3):
            q = 4 * h + 4 + j
            state[0, q : q + 1] = shift[j, 0, h : h + 1] + 0.2 * speed[j, 0, h : h + 1]
            state[1, q : q + 1] = speed[j, 0, h : h + 1]
    first_forces((1, 2), tiles, left, right, homes, shear, bulk, inner, outer, row_in, row_sum, col_sum)
    push[0] = 0.04 * (by_own(row_sum) + by_other(col_sum, 0)) + state[0]
    push[1] = 0.04 * by_other(col_sum, 1)


def relax_body(held, third, shear, len_i, len_o, wgt_i, wgt_o, str_i, str_o, new, mixed, firm):
    def body(at):
        for h in range(2):
            lean, flat = third[h, at], shear[h, at]
            for i in range(3):
                for e in range(3):
                    (length, weight, stretch), n = either((len_i, wgt_i, str_i), (len_o, wgt_o, str_o), i, h, e)
                    m = BLOCKS.index((i, h, e))
                    deviator = stretch[n, at] - lean * length[n, at]
                    one = (0.6 * held[0, h, i, e, at].astype(F32) + 0.4 * deviator).astype(jnp.bfloat16)
                    two = (0.95 * held[1, h, i, e, at].astype(F32) + 0.05 * deviator).astype(jnp.bfloat16)
                    new[0, h, i, e, at] = one
                    new[1, h, i, e, at] = two
                    mixed[m, at] = 0.21 * one.astype(F32) + 0.2375 * two.astype(F32)
                    firm[m, at] = weight[n, at] * flat

    each_chunk(body)


def move(rows, tiles, left, right, pull, i, n):
    for c in range(4):
        t = tile_of(tiles, left, right, i, 0, c)
        rows[4 * n + c, 0:3] = t[0:3] + pull[4 * c : 4 * c + 3] * t[7:8]
        rows[4 * n + c, 3:8] = jnp.zeros((5, N), F32)


def stretches(which, rows, homes, swell_in, swell_out, mixed, firm, inner, outer, stretch_, kernel_, rest_):
    def body(at):
        for h in range(2):
            home = [homes[h, j, at] for j in range(3)]
            swell = jnp.zeros((CHUNK, N), F32) if swell_in is None else swell_in[h, at]
            for q, i in enumerate(which):
                for e in range(3):
                    (length, lever), n = either(inner, outer, i, h, e)
                    t, m, w = 4 * q + h + e, BLOCKS.index((i, h, e)), 6 * q + 3 * h + e
                    gap = [rows[t, j : j + 1] - home[j] for j in range(3)]
                    squared = gap[0] * gap[0] + gap[1] * gap[1] + gap[2] * gap[2]
                    stretch = root(squared) - length[n, at]
                    swell = swell + lever[n, at] * stretch
                    stretch_[w, at] = stretch
                    kernel_[w, at] = firm[m, at] * lax.rsqrt(squared + 0.01)
                    rest_[w, at] = 0.8475 * stretch - mixed[m, at]
            swell_out[h, at] = swell

    each_chunk(body)


def second_body(tiles, left, right, pull, state, mixed, firm, len_i, len_o, lev_i, lev_o, *refs):
    rows, homes, own, swell, stretch, kernel, rest = refs
    for n in range(2):
        move(rows, tiles, left, right, pull[n], 1 + n, n)
    own[0] = pull[0]
    own[1] = state[1] + 5.0 * (pull[0] - state[0])
    for h in range(2):
        spread(homes, h, rows[1 + h], 3)
    stretches((1, 2), rows, homes, None, swell, mixed, firm, (len_i, lev_i), (len_o, lev_o), stretch, kernel, rest)


def second_forces(which, rows, homes, bulk, inner, outer, geo, row_in, row_out, col_sum):
    def force_of(h, at):
        tall = bulk[h, at]

        def force(i, e):
            length, n = either(inner, outer, i, h, e)
            (kernel, rest), w = geo(i, h, e)
            return kernel[w, at] * (length[n, at] * tall + rest[w, at])

        return force

    def place(i, h, e, j):
        ref, n = rows(i)
        return ref[4 * n + h + e, j : j + 1]

    press(which, force_of, place, homes, 0, row_in, row_out, col_sum)


def second_side_body(
    tiles, left, right, pull, mixed, firm, len_i, len_o, lev_i, lev_o, shear, rows, homes, swell, kernel, rest, *refs
):
    push, third, bulk, row_sum, stretch_n, rows_n, kernel_n, rest_n, swl, col_sum = refs
    move(rows_n, tiles, left, right, pull, 0, 0)
    stretches(
        (0,), rows_n, homes, swell, swl, mixed, firm, (len_i, lev_i), (len_o, lev_o), stretch_n, kernel_n, rest_n
    )
    for h in range(2):
        dilatation = 0.4 * shear[h] * jnp.sum(swl[h], axis=1, keepdims=True)
        third[h] = dilatation / 3.0
        bulk[h] = 0.1175 * dilatation

    def geo(i, h, e):
        return (kernel, rest), 6 + 3 * h + e

    second_forces((2,), lambda i: (rows, 1), homes, bulk, len_i, len_o, geo, None, row_sum, col_sum)
    push[...] = by_other(col_sum, 0)


def second_own_body(
    len_i, len_o, bulk, rows, rows_n, homes, kernel, rest, kernel_n, rest_n, row_in, push, row_sum, col_sum
):
    def geo(i, h, e):
        return ((kernel, rest) if i else (kernel_n, rest_n)), 3 * h + e

    second_forces(
        (0, 1), lambda i: (rows if i else rows_n, 0), homes, bulk, len_i, len_o, geo, row_in, row_sum, col_sum
    )
    push[0] = by_other(col_sum, 0)
    push[1] = by_own(row_sum) + by_other(col_sum, 1)


def settle_body(held, third, len_i, len_o, stretch_n, stretch, new):
    def body(at):
        for h in range(2):
            lean = third[h, at]
            for i in range(3):
                for e in range(3):
                    length, n = either(len_i, len_o, i, h, e)
                    longer = stretch[6 * (i - 1) + 3 * h + e, at] if i else stretch_n[3 * h + e, at]
                    deviator = longer - lean * length[n, at]
                    one, two = held[0, h, i, e, at].astype(F32), held[1, h, i, e, at].astype(F32)
                    k = first_offset(i) + e
                    new[0, 0, h, k, at] = (0.6 * one + 0.4 * deviator).astype(jnp.bfloat16)
                    new[1, 0, h, k, at] = (0.95 * two + 0.05 * deviator).astype(jnp.bfloat16)

    each_chunk(body)


def finish_body(total, own, displacement, velocity):
    speed = own[1] + 0.2 * total[...]
    place = own[0] + 0.2 * speed
    for t in range(2):
        for j in range(3):
            q = 4 * (t + 1) + j
            velocity[j, 0, t : t + 1] = speed[q : q + 1]
            displacement[j, 0, t : t + 1] = place[q : q + 1]


def swap_pairs(size, parity):
    return [(i, (i + 1) % size if i % 2 == parity else (i - 1) % size) for i in range(size)]


def row_swaps(slabs, columns):
    pairs = []
    for s in range(slabs):
        for c in range(columns):
            if s in (0, slabs - 1):
                pairs.append((s * columns + c, s * columns + (c ^ 2)))
            else:
                pairs.append((s * columns + c, (s + 1 if s % 2 else s - 1) * columns + c))
    return pairs


def inner_swaps(slabs, columns):
    pairs = []
    for s in range(slabs):
        for c in range(columns):
            if c in (0, columns - 1):
                pairs.append((s * columns + c, (s ^ 1) * columns + c))
            else:
                pairs.append((s * columns + c, s * columns + (c + 1 if c % 2 else c - 1)))
    return pairs


def per_device(slabs, columns, rest_points, tile_fill, displacement, velocity, back_extension):
    s, c = lax.axis_index("slab"), lax.axis_index("col")
    c_odd, low, high = c % 2 == 1, c > 0, c < columns - 1
    inside = (s > 0) & (s < slabs - 1)
    between = low & high
    c_odd, between, inside = lax.optimization_barrier((c_odd, between, inside))
    slab_near, slab_far = swap_pairs(slabs, 0), row_swaps(slabs, columns)
    col_near, col_far = swap_pairs(columns, 0), inner_swaps(slabs, columns)

    def to_near(values):
        return lax.ppermute(values, "slab", slab_near)

    def to_far(values):
        return lax.ppermute(values, ("slab", "col"), slab_far)

    def over_col(to_left, to_right):
        far = lax.ppermute(jnp.where(c_odd, to_right, to_left), ("slab", "col"), col_far)
        near = lax.ppermute(jnp.where(c_odd, to_left, to_right), "col", col_near)
        inland = jnp.where(between, far, 0.0)
        from_left = jnp.where(c_odd, near, inland)
        from_right = jnp.where(c_odd, inland, near)
        return from_left, from_right, near, far

    def add_over_col(sums):
        lo, hi = sums[..., :8, :], sums[..., 8:, :]
        from_left, from_right, _, _ = over_col(lo, hi)
        return jnp.concatenate([lo + from_left, hi + from_right], axis=-2)

    history = jax.ShapeDtypeStruct((2, 2, 3, 3, N, N), back_extension.dtype)
    pages, big = block(2, N, N), block(6, N, N)
    column_sums = [pltpu.VMEM((128 * n, N), F32) for n in range(3)]
    row_sums = pltpu.VMEM((6, N, N), F32)
    hbm = pl.BlockSpec(memory_space=pl.ANY)
    (own,) = call(
        pack_body,
        [block(2, 8, N)],
        (tile_fill, rest_points, displacement),
        scratch=[pltpu.SMEM(tile_fill.shape, jnp.int32)]
        + [pltpu.VMEM(rest_points.shape, F32)] * 2
        + [pltpu.SemaphoreType.DMA((3,))],
        specs=[hbm] * 3,
        limit=None,
    )
    far = to_far(own)
    near = to_near(own)
    held, mixed = call(recall_body, [history, block(18, N, N)], (back_extension,), work=2_000_000)
    near, far, held, mixed = lax.optimization_barrier((near, far, held, mixed))
    tiles = jnp.stack([near, own, jnp.where(inside, far, 0.0)])
    left, right, ghost_near, ghost_far = over_col(tiles[:, 0], tiles[:, 1])
    homes, volume, swell, *inner = call(
        inner_body, [block(2, 7, N, N), pages, pages] + [block(12, N, N)] * 6, (tiles, mixed), work=6_000_000
    )
    three_i = (inner[0], inner[3], inner[4])
    volume, swell, *outer = call(
        functools.partial(outer_body, columns),
        [pages, pages] + [big] * 6,
        (ghost_far, mixed, homes, volume, swell),
        scratch=[pltpu.VMEM((3, 8, N), F32)],
        work=2_000_000,
    )
    push, third, shear, bulk, rows, *outer = call(
        first_body,
        [block(16, N), pages, pages, pages, big] + [big] * 6,
        (tiles, left, right, ghost_near, mixed, homes, volume, swell, *three_i, *outer),
        aliases={11 + k: 5 + k for k in range(6)},
        scratch=[pltpu.VMEM((2, N, N), F32)] * 2 + [column_sums[1]],
        work=4_000_000,
    )
    got = to_near(push)
    push, state = call(
        first_rest_body,
        [block(2, 16, N), block(2, 16, N)],
        (tiles, left, right, homes, displacement, velocity, shear, bulk, rows, *three_i, outer[0], outer[3], outer[4]),
        scratch=[row_sums, column_sums[2]],
        work=4_000_000,
    )
    got, push = lax.optimization_barrier((got, push))
    two = jnp.stack([push[0] + got, push[1]])
    back = to_far(two)
    held, mixed, firm = call(
        relax_body,
        [history, block(18, N, N), block(18, N, N)],
        (held, third, shear, inner[0], outer[0], inner[2], outer[2], inner[5], outer[5]),
        work=4_000_000,
    )
    back, held, mixed, firm = lax.optimization_barrier((back, held, mixed, firm))
    back = jnp.where(inside, back, 0.0)
    pull = add_over_col(two + jnp.stack([back[1], back[0]]))
    pull_near = to_near(pull[0])
    geometry = (mixed, firm, inner[0], outer[0], inner[1], outer[1])
    moved, homes, state, swell, stretch, kernel, rest = call(
        second_body,
        [block(8, 8, N), block(2, 3, N, N), block(2, 16, N), pages] + [block(12, N, N)] * 3,
        (tiles, left, right, pull, state, *geometry),
        work=4_000_000,
    )
    pull_near, swell = lax.optimization_barrier((pull_near, swell))
    push, third, bulk, rows, stretch_near, moved_near, kernel_near, rest_near = call(
        second_side_body,
        [block(16, N), pages, pages, big, big, block(4, 8, N), big, big],
        (tiles, left, right, pull_near, *geometry, shear, moved, homes, swell, kernel, rest),
        scratch=[pltpu.VMEM((2, N, N), F32), column_sums[1]],
        work=4_000_000,
    )
    far = to_far(push)
    (push,) = call(
        second_own_body,
        [block(2, 16, N)],
        (inner[0], outer[0], bulk, moved, moved_near, homes, kernel, rest, kernel_near, rest_near, rows),
        scratch=[row_sums, column_sums[2]],
        work=4_000_000,
    )
    near = to_near(push[0])
    near, far, push = lax.optimization_barrier((near, far, push[1]))
    total = add_over_col(push + near + jnp.where(inside, far, 0.0))
    (held,) = call(
        settle_body,
        [jax.ShapeDtypeStruct(back_extension.shape, back_extension.dtype)],
        (held, third, inner[0], outer[0], stretch_near, stretch),
        work=3_000_000,
    )
    shape = block(*rest_points.shape)
    displacement, velocity = call(finish_body, [shape, shape], (total, state))
    return (displacement, velocity, held)


def solution(mesh):
    in_specs = (
        P(None, "slab", "col", None),
        P("slab", "col"),
        P(None, "slab", "col", None),
        P(None, "slab", "col", None),
        P(None, "slab", "col", None, None, None),
    )
    out_specs = (
        P(None, "slab", "col", None),
        P(None, "slab", "col", None),
        P(None, "slab", "col", None, None, None),
    )
    return jax.shard_map(
        functools.partial(per_device, mesh.shape["slab"], mesh.shape["col"]),
        mesh=mesh,
        in_specs=in_specs,
        out_specs=out_specs,
        check_vma=False,
    )
```
